32 devices in a mesh: groups: 2 (over x), cache: 16 (over z, y, core).
Axes of the slice: x: 2, y: 2, z: 4, core: 2. Of those that a mesh axis runs over, the one named last changes fastest.
Arguments:
- prefix_len: int32 [32], P('groups'), parts along dimension 0, may hold values from 128 to 1024, as said below
- hits: int32 [32, 1], P('groups'), parts along dimension 0, may hold values from 0 to 15, as said below
- span_block: int32 [32, 16], P('groups'), parts along dimension 0, may hold values from 0 to 15, each once within a row
- queries: bfloat16 [2048, 2048], P(('groups', 'cache')), parts along dimension 0, may hold values from -100 to 100
- fresh_keys: bfloat16 [2048, 128], P(('groups', 'cache')), parts along dimension 0, may hold values from -4 to 4
- fresh_values: bfloat16 [2048, 128], P(('groups', 'cache')), parts along dimension 0, may hold values from -4 to 4
- cache_keys: bfloat16 [65536, 128], P(('groups', 'cache')), parts along dimension 0, may hold values from -4 to 4
- cache_values: bfloat16 [65536, 128], P(('groups', 'cache')), parts along dimension 0, may hold values from -4 to 4
Outputs:
- attended: bfloat16 [2048, 2048], P(('groups', 'cache')), parts along dimension 0
The draws below stay inside these ranges and needn't reach their ends.
There are 2 independent parts, one for each index of `groups`. The reference program is written for one: setup_inputs(seed, part) draws one part's arguments, and reference() takes and returns one part's arrays. A program takes and returns all parts, laid end to end along the dimension named above; each array names one. Nothing has to cross between parts.
Inputs may be any that keep to these rules, and one draw needn't show every extreme that they name: `prefix_len`: every request's prefix holds at least 128 tokens, and one request in every draw holds exactly 1024. `hits`: each row names 1 different devices. Each device is named by at most 2 requests; 4 devices are named by exactly 2, half of them by one, a quarter by none. `span_block`: each row is a permutation.
All inputs are finite; a program needn't handle non-finite values.
Results may differ from the reference program's by a relative error of at most 0.0065.
Values may be sent and summed in bfloat16 or wider, within the bound.
A program may use at most 64 MiB of HBM per device.

```python
import jax
import jax.numpy as jnp
from jax import lax

HEADS = 16
HD = 128
PAGE = 128
CAP = 2
REQUESTS = 16
TOK_REQ = 4
PAGES_DEV = 16
HITS = 1
TOKENS = 1024
CACHE_ROWS = 32768
PREFIX = 1024
N_CACHE = 16


def hit_table(key):
    seeded = jax.random.fold_in(key, 101)
    shuffled = jax.random.permutation(jax.random.fold_in(seeded, 1), N_CACHE)
    doubled = N_CACHE // 4
    listing = jnp.concatenate([shuffled[:N_CACHE - doubled], shuffled[:doubled]]).reshape(REQUESTS, HITS)
    row_order = jax.random.permutation(jax.random.fold_in(seeded, 2), REQUESTS)
    listing = jnp.take(listing, row_order, axis=0)
    row_keys = jax.random.split(jax.random.fold_in(seeded, 3), REQUESTS)

    def one_order(row_key):
        return jax.random.permutation(row_key, HITS)
    col_order = jax.vmap(one_order)(row_keys)
    return jnp.take_along_axis(listing, col_order, axis=1).astype(jnp.int32)


def paired_table(key, count, salt):
    drawn_values = jax.random.normal(jax.random.fold_in(key, salt + 2), (count, HD), jnp.float32)
    return jnp.clip(drawn_values, -4.0, 4.0)


def draw_prefix_len(key, part):
    lengths = jax.random.randint(jax.random.fold_in(key, 202), (REQUESTS,), PREFIX // 8, PREFIX + 1)
    longest = jax.random.randint(jax.random.fold_in(key, 203), (), 0, REQUESTS)
    return lengths.at[longest].set(PREFIX).astype(jnp.int32)


def draw_hits(key, part):
    return hit_table(key)


def draw_fresh_keys(key, part):
    return paired_table(key, TOKENS, 301).astype(jnp.bfloat16)


def draw_cache_keys(key, part):
    return paired_table(key, CACHE_ROWS, 311).astype(jnp.bfloat16)


def draw_queries(key, part):
    drawn_values = jnp.clip(jax.random.normal(jax.random.fold_in(key, 402), (TOKENS, HEADS, HD), jnp.float32), -4.0, 4.0)
    return drawn_values.reshape(TOKENS, HEADS * HD).astype(jnp.bfloat16)


def level_of(stream_key, shape, cuts, low, top_value):
    loudness, own = 1.0, jax.random.fold_in(stream_key, 6)
    for axis_at, blocks in cuts:
        steps = jnp.exp(jax.random.uniform(jax.random.fold_in(own, axis_at), (blocks,), jnp.float32, low / len(cuts), top_value / len(cuts)))
        loudness = loudness * jnp.repeat(steps, shape[axis_at] // blocks).reshape([-1 if axis == axis_at else 1 for axis in range(len(shape))])
    return loudness


def normal_values(key, shape, scale, most, pieces=(), held_as=jnp.bfloat16):
    values = scale * jax.random.normal(key, shape, jnp.float32)
    if pieces:
        values = values * level_of(key, shape, pieces, -0.22, 0.18)
    return jnp.clip(values, -most, most).astype(held_as)


def setup_inputs(seed: int = 0, part: int = 0) -> dict:
    keys = jax.random.split(jax.random.key(seed), 9)
    part_keys = jax.random.split(jax.random.fold_in(keys[8], part), 9)
    prefix_len = draw_prefix_len(jax.random.fold_in(jax.random.fold_in(keys[8], part), 71), part)
    hits = draw_hits(jax.random.fold_in(jax.random.fold_in(keys[8], part), 71), part)
    span_block = jax.vmap(lambda own: jax.random.permutation(own, N_CACHE))(jax.random.split(part_keys[2], REQUESTS)).reshape((REQUESTS, N_CACHE)).astype(jnp.int32)
    queries = draw_queries(jax.random.fold_in(jax.random.fold_in(keys[8], part), 71), part)
    fresh_keys = draw_fresh_keys(jax.random.fold_in(jax.random.fold_in(keys[8], part), 71), part)
    fresh_values = normal_values(part_keys[5], (TOKENS, HD), 1.0, 4.0, ((0, 16),))
    cache_keys = draw_cache_keys(jax.random.fold_in(jax.random.fold_in(keys[8], part), 71), part)
    cache_values = normal_values(part_keys[7], (CACHE_ROWS, HD), 1.0, 4.0, ((0, 16),))
    return {"prefix_len": prefix_len, "hits": hits, "span_block": span_block, "queries": queries, "fresh_keys": fresh_keys, "fresh_values": fresh_values, "cache_keys": cache_keys, "cache_values": cache_values}


floor_score = -1e30


def attend(query_rows, key_rows, value_rows, visible, rounding):
    scale = HD ** -0.5
    scores = jnp.einsum("qhd,kd->qhk", query_rows, key_rows, precision=lax.Precision.HIGHEST) * scale
    scores = jnp.where(visible[:, None, :], scores, floor_score)
    maxima = jnp.max(scores, axis=2)
    weights = jnp.exp(scores - maxima[:, :, None]) * visible[:, None, :]
    totals = jnp.sum(weights, axis=2)
    if rounding:
        weights = lax.optimization_barrier(weights.astype(jnp.bfloat16)).astype(jnp.float32)
    summed = jnp.einsum("qhk,kd->qhd", weights, value_rows, precision=lax.Precision.HIGHEST)
    return maxima, totals, summed


def reference(prefix_len, hits, span_block, queries, fresh_keys, fresh_values, cache_keys, cache_values):
    region = (PAGES_DEV // CAP) * PAGE
    per_device = REQUESTS * TOK_REQ
    matches = jnp.any(hits[:, :, None, None] == hits[None, None, :, :], axis=3)
    earlier = jnp.arange(REQUESTS)[None, None, :] < jnp.arange(REQUESTS)[:, None, None]
    slot_rank = jnp.sum(matches & earlier, axis=2).astype(jnp.int32)
    offsets = jnp.arange(TOK_REQ, dtype=jnp.int32)
    devices = jnp.arange(N_CACHE, dtype=jnp.int32)
    spots = jnp.arange(region, dtype=jnp.int32)

    def one_request(request):
        row_index = (devices[:, None] * per_device + request * TOK_REQ + offsets[None, :]).reshape(-1).astype(jnp.int32)
        query_rows = jnp.take(queries, row_index, axis=0).astype(jnp.float32).reshape(-1, HEADS, HD)
        key_rows = jnp.take(fresh_keys, row_index, axis=0).astype(jnp.float32)
        value_rows = jnp.take(fresh_values, row_index, axis=0).astype(jnp.float32)
        positions = (span_block[request][:, None] * TOK_REQ + offsets[None, :]).reshape(-1)
        causal = positions[None, :] <= positions[:, None]
        maxima, totals, summed = attend(query_rows, key_rows, value_rows, causal, False)
        prompt_out = summed / totals[:, :, None]
        prompt_lse = maxima + jnp.log(totals)

        def one_owner(which):
            owner = hits[request, which]
            start = (owner * PAGES_DEV * PAGE + slot_rank[request, which] * region).astype(jnp.int32)
            page_keys = lax.dynamic_slice_in_dim(cache_keys, start, region, 0).astype(jnp.float32)
            page_values = lax.dynamic_slice_in_dim(cache_values, start, region, 0).astype(jnp.float32)
            visible = ((which * region + spots) < prefix_len[request])[None, :]
            owner_max, owner_total, owner_sum = attend(query_rows, page_keys, page_values, visible, True)
            owner_total = jnp.maximum(owner_total, 1.0)
            owner_out = (owner_sum / owner_total[:, :, None]).astype(jnp.bfloat16)
            return owner_out, owner_max + jnp.log(owner_total)

        owner_out, owner_lse = lax.map(one_owner, jnp.arange(HITS, dtype=jnp.int32))
        owner_wide = lax.optimization_barrier(owner_out).astype(jnp.float32)
        every_lse = jnp.concatenate([prompt_lse[None], owner_lse], axis=0)
        highest = jnp.max(every_lse, axis=0)
        shares = jnp.exp(every_lse - highest[None])
        combined = shares[0][:, :, None] * prompt_out + jnp.sum(shares[1:][:, :, :, None] * owner_wide, axis=0)
        result = combined / jnp.sum(shares, axis=0)[:, :, None]
        return result.astype(jnp.bfloat16).reshape(N_CACHE, TOK_REQ, HEADS * HD)

    blocks = lax.map(one_request, jnp.arange(REQUESTS, dtype=jnp.int32))
    return jnp.transpose(blocks, (1, 0, 2, 3)).reshape(N_CACHE * per_device, HEADS * HD)
```

```python
import functools
import math

import jax
import jax.numpy as jnp
from jax import lax
from jax.experimental import pallas as pl
from jax.experimental.pallas import tpu as pltpu
from jax.sharding import PartitionSpec as P

HEADS = 16
HD = 128
PAGE = 128
CAP = 2
REQUESTS = 16
TOK = 4
PAGES_DEV = 16
REGION = PAGES_DEV // CAP * PAGE
PER_DEV = REQUESTS * TOK
PLANE = 4
ROWS = PLANE * TOK * HEADS
MESH = pl.DeviceIdType.MESH
FLOOR = -1e30
EXP2_SCALE = HD**-0.5 * math.log2(math.e)


def flip(a, b, size):
    out, bit = 0, 1
    while bit < size:
        out = out + ((a // bit + b // bit) % 2) * bit
        bit *= 2
    return out


def attend(q, k, v, visible):
    s = lax.dot_general(q, k, (((1,), (1,)), ((), ())), preferred_element_type=jnp.float32)
    s = jnp.where(visible, s, FLOOR)
    m = jnp.max(s, axis=1, keepdims=True)
    p = jnp.exp2((s - m) * EXP2_SCALE).astype(jnp.bfloat16)
    v1 = jnp.concatenate([v, jnp.ones_like(v)], axis=1)
    o = jnp.dot(p, v1, preferred_element_type=jnp.float32)
    return m, o


def head_lanes(x, units, first):
    row = lax.broadcasted_iota(jnp.int32, (units, TOK * HEADS, HD), 1)
    lane = lax.broadcasted_iota(jnp.int32, (units, TOK * HEADS, HD), 2)
    wide = x.reshape(units, TOK * HEADS, HD)
    return jnp.sum(jnp.where(row + first == lane, wide, 0.0), axis=1)


def head_rows(x, units):
    row = lax.broadcasted_iota(jnp.int32, (units, TOK * HEADS, HD), 1)
    lane = lax.broadcasted_iota(jnp.int32, (units, TOK * HEADS, HD), 2)
    wide = jnp.broadcast_to(x[:, None, :], (units, TOK * HEADS, HD))
    return jnp.sum(jnp.where(row == lane, wide, 0.0), axis=2, keepdims=True)


def mirrored(a, size):
    out, bit = 0, 1
    while bit < size:
        out = out + ((a // bit) % 2) * (size // (2 * bit))
        bit *= 2
    return out


def kernel(n, hit_count, prefix, hits, span, queries, fk, fv, ck, cv, out,
           qin, qx, send, arrived, ret, back, lret, lback, kv, kc, vc, pout, plse, comb, lcomb,
           qs, qr, rs, rr, ls, lr, s1s, s1r, loc):
    me = lax.axis_index("cache")
    planes = n // PLANE
    stages = int(math.log2(n))
    spot_me = mirrored(me, n)
    my_plane = me // PLANE

    loads = [
        pltpu.make_async_copy(queries, qin, loc.at[4]),
        pltpu.make_async_copy(fk, kv.at[spot_me, 0], loc.at[0]),
        pltpu.make_async_copy(fv, kv.at[spot_me, 1], loc.at[1]),
        pltpu.make_async_copy(ck, kc, loc.at[2]),
        pltpu.make_async_copy(cv, vc, loc.at[3]),
    ]
    for load in loads:
        load.start()

    barrier = pltpu.get_barrier_semaphore()

    @pl.loop(1, n)
    def _(k):
        pl.semaphore_signal(barrier, inc=1, device_id={"cache": (me + k) % n}, device_id_type=MESH)

    def named_by(d):
        first = jnp.int32(REQUESTS - 1)
        last = jnp.int32(0)
        for r in range(REQUESTS):
            for i in range(hit_count):
                here = hits[r * hit_count + i] == d
                first = jnp.where(here, jnp.minimum(first, r), first)
                last = jnp.where(here, r, last)
        return first, last

    loads[0].wait()
    qx[...] = qin[...].reshape(REQUESTS, TOK, HEADS, HD)

    @pl.loop(0, n)
    def _(d):
        first, last = named_by(d)
        send[d, 0] = qx[first]
        send[d, 1] = qx[last]

    pl.semaphore_wait(barrier, n - 1)
    loads[1].wait()
    loads[2].wait()

    def kv_copy(t, mine=True):
        size = 2**t
        start = (spot_me // size) * size
        if not mine:
            start = flip(spot_me // size, 1, n // size) * size
        block = kv.at[pl.ds(start, size)]
        return pltpu.make_async_remote_copy(
            src_ref=block, dst_ref=block, send_sem=s1s.at[t], recv_sem=s1r.at[t],
            device_id={"cache": flip(me, n // (2 * size), n)}, device_id_type=MESH)

    kv_copy(0).start()

    def query_copy(to, frm):
        return pltpu.make_async_remote_copy(
            src_ref=send.at[to], dst_ref=arrived.at[frm], send_sem=qs.at[to], recv_sem=qr.at[frm],
            device_id={"cache": to}, device_id_type=MESH)

    def out_copy(to, frm):
        return pltpu.make_async_remote_copy(
            src_ref=ret.at[to], dst_ref=back.at[frm], send_sem=rs.at[to], recv_sem=rr.at[frm],
            device_id={"cache": to}, device_id_type=MESH)

    def lse_copy(to, frm):
        return pltpu.make_async_remote_copy(
            src_ref=lret.at[to], dst_ref=lback.at[frm], send_sem=ls.at[to], recv_sem=lr.at[frm],
            device_id={"cache": to}, device_id_type=MESH)

    def peers(j, act):
        base = flip(my_plane, j, planes) * PLANE

        @pl.loop(0, PLANE)
        def _(k):
            d = base + (me + k) % PLANE

            @pl.when(d != me)
            def _():
                act(d)

    @pl.loop(0, planes)
    def _(i):
        peers((i + 1) % planes, lambda d: query_copy(d, me).start())

    arrived[me] = send[me]
    loads[3].wait()
    loads[4].wait()

    limits = []
    for request in named_by(me):
        place = jnp.int32(0)
        for i in range(hit_count):
            place = jnp.where(hits[request * hit_count + i] == me, i, place)
        limits.append(prefix[request] - place * REGION)
    spot = lax.broadcasted_iota(jnp.int32, (1, REGION), 1)

    def serve(j):
        peers(j, lambda d: query_copy(d, d).wait_recv())
        base = flip(my_plane, j, planes) * PLANE
        lanes = jnp.zeros((PLANE, HD), jnp.float32)

        for slot in range(CAP):
            q = arrived[pl.ds(base, PLANE), slot].reshape(ROWS, HD)
            part = pl.ds(slot * REGION, REGION)
            m, o = attend(q, kc[part], vc[part], spot < limits[slot])
            total = jnp.maximum(o[:, HD:], 1.0)
            lse = m * EXP2_SCALE + jnp.log2(total)
            lse = jnp.where(limits[slot] > 0, lse, FLOOR)
            result = (o[:, :HD] / total).astype(jnp.bfloat16)
            ret[pl.ds(base, PLANE), slot] = result.reshape(PLANE, TOK, HEADS, HD)
            lanes = lanes + head_lanes(lse, PLANE, slot * TOK * HEADS)
        for k in range(PLANE):
            lret[base + k] = lanes[k:k + 1]

        def go(d):
            out_copy(d, me).start()
            lse_copy(d, me).start()

        peers(j, go)

        for t in range(stages - 1):
            @pl.when(j == t)
            def _():
                kv_copy(t, mine=False).wait_recv()
                kv_copy(t + 1).start()

    pl.loop(0, planes)(serve)
    back[me] = ret[me]
    lback[me] = lret[me]
    kv_copy(stages - 1, mine=False).wait_recv()

    span_f = span[...].astype(jnp.float32)
    mine = jnp.sum(
        jnp.where(lax.broadcasted_iota(jnp.int32, span_f.shape, 1) == me, span_f, 0.0),
        axis=1, keepdims=True)
    order = jnp.clip(span_f - mine, -1.0, 1.0).astype(jnp.bfloat16)
    group = 16
    keys = group * PER_DEV
    chunks = n // group
    key_lane = lax.broadcasted_iota(jnp.int32, (REQUESTS, keys), 1)
    key_row = lax.broadcasted_iota(jnp.int32, (REQUESTS, keys), 0)

    def ranks(chunk):
        lane = lax.broadcasted_iota(jnp.int32, (n, keys), 1)
        dev = lax.broadcasted_iota(jnp.int32, (n, keys), 0)
        pick = jnp.where(mirrored(lane // PER_DEV + chunk * group, n) == dev, 1.0, 0.0).astype(jnp.bfloat16)
        step = jnp.dot(order, pick, preferred_element_type=jnp.float32)
        spot_rank = step * TOK + (key_lane % TOK).astype(jnp.float32)
        same = (key_lane // TOK) % REQUESTS == key_row
        return jnp.where(same, spot_rank, 100.0).astype(jnp.bfloat16)

    def kv_rows(chunk, which):
        return kv[pl.ds(chunk * group, group), which].reshape(keys, HD)

    def prompt_part(c, chunk, rank):
        q = qx_rows(c)
        row = lax.broadcasted_iota(jnp.int32, (ROWS, REQUESTS), 0)
        req = lax.broadcasted_iota(jnp.int32, (ROWS, REQUESTS), 1)
        spread = jnp.where(row // (TOK * HEADS) + c * (ROWS // (TOK * HEADS)) == req, 1.0, 0.0)
        ranked = jnp.dot(spread.astype(jnp.bfloat16), rank, preferred_element_type=jnp.float32)
        token = (lax.broadcasted_iota(jnp.int32, (ROWS, 1), 0) // HEADS) % TOK
        return attend(q, kv_rows(chunk, 0), kv_rows(chunk, 1), ranked <= token.astype(jnp.float32))

    reqs = ROWS // (TOK * HEADS)

    def qx_rows(c):
        return qx[pl.ds(c * reqs, reqs)].reshape(ROWS, HD)

    rank0 = ranks(0) if chunks == 1 else None

    @pl.loop(0, REQUESTS // reqs)
    def _(c):
        if chunks == 1:
            m, o = prompt_part(c, 0, rank0)
        else:
            def more(chunk, carry):
                m0, o0 = carry
                m1, o1 = prompt_part(c, chunk, ranks(chunk))
                m2 = jnp.maximum(m0, m1)
                return m2, (o0 * jnp.exp2((m0 - m2) * EXP2_SCALE)
                            + o1 * jnp.exp2((m1 - m2) * EXP2_SCALE))
            m, o = lax.fori_loop(0, chunks, more, (
                jnp.full((ROWS, 1), FLOOR, jnp.float32), jnp.zeros((ROWS, 2 * HD), jnp.float32)))
        total = o[:, HD:]
        pout[pl.ds(c * reqs, reqs)] = (o[:, :HD] / total).reshape(reqs, TOK, HEADS, HD)
        plse[pl.ds(pl.multiple_of(c * reqs, reqs), reqs)] = head_lanes(m * EXP2_SCALE + jnp.log2(total), reqs, 0)

    def finish(d):
        out_copy(d, d).wait_recv()
        lse_copy(d, d).wait_recv()

    pl.loop(0, planes)(lambda j: peers(j, finish))

    for i in range(hit_count):
        for r in range(REQUESTS):
            owner = hits[r * hit_count + i]
            rank = jnp.int32(0)
            for r2 in range(r):
                for i2 in range(hit_count):
                    rank = jnp.where(hits[r2 * hit_count + i2] == owner, rank + 1, rank)
            rank = jnp.minimum(rank, CAP - 1)
            comb[i, r] = back[owner, rank]
            row = lback[owner]
            lcomb[i, r:r + 1] = jnp.where(rank == 0, row, pltpu.roll(row, HD // 2, 1))

    top = plse[...]
    for i in range(hit_count):
        top = jnp.maximum(top, lcomb[i])
    share = jnp.exp2(plse[...] - top)
    shares = [jnp.exp2(lcomb[i] - top) for i in range(hit_count)]
    scale = 1.0 / functools.reduce(jnp.add, shares, share)
    whole = (REQUESTS, TOK * HEADS, HD)
    mixed = head_rows(share * scale, REQUESTS) * pout[...].reshape(whole)
    for i in range(hit_count):
        mixed = mixed + head_rows(shares[i] * scale, REQUESTS) * comb[i].reshape(whole).astype(jnp.float32)
    out[...] = mixed.astype(jnp.bfloat16).reshape(PER_DEV, HEADS, HD)

    def drained(d):
        query_copy(d, me).wait_send()
        out_copy(d, me).wait_send()
        lse_copy(d, me).wait_send()

    pl.loop(0, planes)(lambda j: peers(j, drained))
    for t in range(stages):
        kv_copy(t).wait_send()


def toggle(a, mask):
    out, bit = a, 1
    while bit <= mask:
        if mask & bit:
            out = out + bit - 2 * bit * ((a // bit) % 2)
        bit *= 2
    return out


def relay_kernel(n, prefix, hits, span, queries, fk, fv, ck, cv, out,
                 qin, qx, near_s, far_s, pack_s, near_in, far_in, pack_in, fwd, rel_in,
                 near_o, far_o, rel_o, relr, packr, back, near_l, far_l, rel_l, relr_l, packr_l, lback,
                 kv, kc, vc, pout, plse, comb, lcomb, firsts, lasts, doubled, chosen, owners, places,
                 nqs, nqr, fqs, fqr, wqs, wqr, nrs, nrr, frs, frr, wrs, wrr,
                 nls, nlr, fls, flr, wls, wlr, pqs, pqr, prs, prr, pls, plr, s1s, s1r, loc):
    me = lax.axis_index("cache")
    half = n // 2
    doubles = n // 4
    low = me % half
    side = me // half
    other = toggle(me, half)
    stages = int(math.log2(n))
    spot_me = mirrored(me, n)
    my_plane = (low // PLANE) * PLANE
    near_far = 2 * half
    packed = 3 * half

    loads = [
        pltpu.make_async_copy(queries, qin, loc.at[4]),
        pltpu.make_async_copy(fk, kv.at[spot_me, 0], loc.at[0]),
        pltpu.make_async_copy(fv, kv.at[spot_me, 1], loc.at[1]),
        pltpu.make_async_copy(ck, kc, loc.at[2]),
        pltpu.make_async_copy(cv, vc, loc.at[3]),
    ]
    for load in loads:
        load.start()

    barrier = pltpu.get_barrier_semaphore()
    for mask in reversed(range(1, n)):
        pl.semaphore_signal(barrier, inc=1, device_id={"cache": toggle(me, mask)}, device_id_type=MESH)

    for part in range(2):
        seen = jnp.int32(0)
        picks = [jnp.int32(0)] * doubles
        lows = [jnp.int32(0)] * doubles
        for spot in range(half):
            d = part * half + spot
            first = jnp.int32(REQUESTS - 1)
            last = jnp.int32(0)
            for r in reversed(range(REQUESTS)):
                first = jnp.where(hits[r] == d, r, first)
            for r in range(REQUESTS):
                last = jnp.where(hits[r] == d, r, last)
            firsts[d] = first
            lasts[d] = last
            doubled[d] = jnp.minimum(seen, doubles - 1)
            two = first < last
            for j in range(doubles):
                here = two & (seen == j)
                picks[j] = jnp.where(here, last, picks[j])
                lows[j] = jnp.where(here, spot, lows[j])
            seen = jnp.where(two, seen + 1, seen)
        for j in range(doubles):
            chosen[part * doubles + j] = picks[j]
            owners[part * doubles + j] = lows[j]

    for r in range(REQUESTS):
        owner = hits[r]
        second = firsts[owner] < r
        at_low = owner % half
        inside = 2 * at_low + jnp.where(second, 1, 0)
        outside = jnp.where(second, packed + doubled[owner], near_far + at_low)
        places[r] = jnp.where(owner // half == side, inside, outside)

    loads[0].wait()
    qx[...] = qin[...].reshape(REQUESTS, TOK, HEADS, HD)
    for j in range(doubles):
        pack_s[j] = qx[chosen[(1 - side) * doubles + j]]

    @pl.loop(0, half)
    def _(d):
        near_s[d, 0] = qx[firsts[side * half + d]]
        near_s[d, 1] = qx[lasts[side * half + d]]
        far_s[d] = qx[firsts[(1 - side) * half + d]]

    near_in[low] = near_s[low]
    for load in loads[1:]:
        load.wait()
    pl.semaphore_wait(barrier, n - 1)

    def remote(src, dst, sent, got, to):
        return pltpu.make_async_remote_copy(
            src_ref=src, dst_ref=dst, send_sem=sent, recv_sem=got,
            device_id={"cache": to}, device_id_type=MESH)

    def kv_copy(t, mine=True):
        size = 2**t
        start = (spot_me // size) * size
        if not mine:
            start = flip(spot_me // size, 1, n // size) * size
        block = kv.at[pl.ds(start, size)]
        return remote(block, block, s1s.at[t], s1r.at[t], toggle(me, n // (2 * size)))

    def inner(d):
        return side * half + d

    def outer(d):
        return (1 - side) * half + d

    def near_query(to, frm):
        return remote(near_s.at[to], near_in.at[frm], nqs.at[to], nqr.at[frm], inner(to))

    def far_query(to, frm):
        return remote(far_s.at[to], far_in.at[frm], fqs.at[to], fqr.at[frm], outer(to))

    def relay_query(to, frm):
        return remote(fwd.at[to], rel_in.at[frm], wqs.at[to], wqr.at[frm], inner(to))

    def near_out(to, frm):
        return (remote(near_o.at[to], back.at[pl.ds(2 * frm, 2)], nrs.at[to], nrr.at[frm], inner(to)),
                remote(near_l.at[to], lback.at[pl.ds(2 * frm, 2)], nls.at[to], nlr.at[frm], inner(to)))

    def far_out(to, frm):
        return (remote(far_o.at[to], back.at[near_far + frm], frs.at[to], frr.at[frm], outer(to)),
                remote(far_l.at[to], lback.at[near_far + frm], fls.at[to], flr.at[frm], outer(to)))

    def relay_out(to, frm):
        return (remote(rel_o.at[to], relr.at[frm], wrs.at[to], wrr.at[frm], inner(to)),
                remote(rel_l.at[to], relr_l.at[frm], wls.at[to], wlr.at[frm], inner(to)))

    pack_query = remote(pack_s, pack_in, pqs.at[0], pqr.at[0], other)
    pack_out = (remote(packr, back.at[pl.ds(packed, doubles)], prs.at[0], prr.at[0], other),
                remote(packr_l, lback.at[pl.ds(packed, doubles)], pls.at[0], plr.at[0], other))

    near_masks = list(range(1, half))
    plane_masks = list(range(1, PLANE))
    cross_masks = list(range(PLANE, half))

    pack_query.start()
    kv_copy(0).start()
    for mask in range(half):
        far_query(toggle(low, mask), low).start()
    for mask in near_masks:
        near_query(toggle(low, mask), low).start()

    limits = [prefix[firsts[me]], prefix[lasts[me]]]
    spot = lax.broadcasted_iota(jnp.int32, (1, REGION), 1)

    def answer(q, slot):
        part = pl.ds(slot * REGION, REGION)
        m, o = attend(q.reshape(ROWS, HD), kc[part], vc[part], spot < limits[slot])
        total = jnp.maximum(o[:, HD:], 1.0)
        lse = m * EXP2_SCALE + jnp.log2(total)
        result = (o[:, :HD] / total).astype(jnp.bfloat16)
        return result.reshape(PLANE, TOK, HEADS, HD), head_lanes(lse, PLANE, 0)

    def near_group(base, masks):
        for mask in masks:
            d = toggle(low, mask)
            near_query(d, d).wait_recv()
        group = pl.ds(base, PLANE)
        for slot in range(CAP):
            result, lanes = answer(near_in[group, slot], slot)
            near_o[group, slot] = result
            for k in range(PLANE):
                near_l[base + k, slot] = lanes[k:k + 1]
        for mask in masks:
            for copy in near_out(toggle(low, mask), low):
                copy.start()

    def far_group(base, masks):
        for mask in masks:
            d = toggle(low, mask)
            far_query(d, d).wait_recv()
        group = pl.ds(base, PLANE)
        result, lanes = answer(far_in[group], 0)
        far_o[group] = result
        for k in range(PLANE):
            far_l[base + k] = lanes[k:k + 1]
        for mask in masks:
            for copy in far_out(toggle(low, mask), low):
                copy.start()

    def relay_group(base, masks):
        for mask in masks:
            d = toggle(low, mask)
            relay_query(d, d).wait_recv()
        group = pl.ds(base, PLANE)
        result, lanes = answer(rel_in[group], 1)
        rel_o[group] = result
        for k in range(PLANE):
            rel_l[base + k] = lanes[k:k + 1]
        for mask in masks:
            for copy in relay_out(toggle(low, mask), low):
                copy.start()

    def next_kv(t):
        kv_copy(t, mine=False).wait_recv()
        kv_copy(t + 1).start()

    plane_next = toggle(low, PLANE) // PLANE * PLANE
    near_group(my_plane, plane_masks)
    back[pl.ds(2 * low, 2)] = near_o[low]
    lback[pl.ds(2 * low, 2)] = near_l[low]

    pack_query.wait_recv()

    @pl.loop(0, half)
    def _(d):
        fwd[d] = pack_in[doubled[side * half + d]]

    rel_in[low] = fwd[low]
    for mask in near_masks:
        relay_query(toggle(low, mask), low).start()
    next_kv(0)
    near_group(plane_next, cross_masks)
    far_group(my_plane, [0] + plane_masks)
    next_kv(1)
    relay_group(my_plane, plane_masks)
    relr[low] = rel_o[low]
    relr_l[low] = rel_l[low]
    relay_group(plane_next, cross_masks)
    far_group(plane_next, cross_masks)
    next_kv(2)

    for mask in near_masks:
        d = toggle(low, mask)
        for copy in relay_out(d, d):
            copy.wait_recv()
    for j in range(doubles):
        packr[j] = relr[owners[side * doubles + j]]
        packr_l[j] = relr_l[owners[side * doubles + j]]
    for copy in pack_out:
        copy.start()

    kv_copy(stages - 1, mine=False).wait_recv()
    span_f = span[...].astype(jnp.float32)
    mine = jnp.sum(
        jnp.where(lax.broadcasted_iota(jnp.int32, span_f.shape, 1) == me, span_f, 0.0),
        axis=1, keepdims=True)
    order = jnp.clip(span_f - mine, -1.0, 1.0).astype(jnp.bfloat16)
    reqs = ROWS // (TOK * HEADS)
    rows = reqs * TOK
    keys = n * rows
    key_lane = lax.broadcasted_iota(jnp.int32, (REQUESTS, keys), 1)
    key_row = lax.broadcasted_iota(jnp.int32, (REQUESTS, keys), 0)
    lane = lax.broadcasted_iota(jnp.int32, (n, keys), 1)
    dev = lax.broadcasted_iota(jnp.int32, (n, keys), 0)
    pick = jnp.where(mirrored(lane // rows, n) == dev, 1.0, 0.0).astype(jnp.bfloat16)
    step = jnp.dot(order, pick, preferred_element_type=jnp.float32)
    rank_all = step * TOK + (key_lane % TOK).astype(jnp.float32)
    token = ((lax.broadcasted_iota(jnp.int32, (ROWS, 1), 0) // HEADS) % TOK).astype(jnp.float32)
    row_at = lax.broadcasted_iota(jnp.int32, (ROWS, REQUESTS), 0) // (TOK * HEADS)
    req_at = lax.broadcasted_iota(jnp.int32, (ROWS, REQUESTS), 1)

    @pl.loop(0, REQUESTS // reqs)
    def _(c):
        same = (key_lane // TOK) % reqs + c * reqs == key_row
        rank = jnp.where(same, rank_all, 100.0).astype(jnp.bfloat16)
        spread = jnp.where(row_at + c * reqs == req_at, 1.0, 0.0).astype(jnp.bfloat16)
        ranked = jnp.dot(spread, rank, preferred_element_type=jnp.float32)
        part = pl.ds(pl.multiple_of(c * rows, rows), rows)
        m, o = attend(qx[pl.ds(c * reqs, reqs)].reshape(ROWS, HD), kv[:, 0, part].reshape(keys, HD),
                      kv[:, 1, part].reshape(keys, HD), ranked <= token)
        total = o[:, HD:]
        pout[pl.ds(c * reqs, reqs)] = (o[:, :HD] / total).reshape(reqs, TOK, HEADS, HD)
        plse[pl.ds(pl.multiple_of(c * reqs, reqs), reqs)] = head_lanes(m * EXP2_SCALE + jnp.log2(total), reqs, 0)

    for mask in near_masks:
        d = toggle(low, mask)
        for copy in near_out(d, d):
            copy.wait_recv()
    for mask in range(half):
        d = toggle(low, mask)
        for copy in far_out(d, d):
            copy.wait_recv()
    for copy in pack_out:
        copy.wait_recv()

    for r in range(REQUESTS):
        comb[r] = back[places[r]]
        lcomb[r:r + 1] = lback[places[r]]
    top = jnp.maximum(plse[...], lcomb[...])
    share = jnp.exp2(plse[...] - top)
    taken = jnp.exp2(lcomb[...] - top)
    scale = 1.0 / (share + taken)
    whole = (REQUESTS, TOK * HEADS, HD)
    mixed = head_rows(share * scale, REQUESTS) * pout[...].reshape(whole)
    mixed = mixed + head_rows(taken * scale, REQUESTS) * comb[...].reshape(whole).astype(jnp.float32)
    out[...] = mixed.astype(jnp.bfloat16).reshape(PER_DEV, HEADS, HD)

    pack_query.wait_send()
    for mask in range(half):
        d = toggle(low, mask)
        far_query(d, low).wait_send()
        for copy in far_out(d, low):
            copy.wait_send()
    for mask in near_masks:
        d = toggle(low, mask)
        near_query(d, low).wait_send()
        relay_query(d, low).wait_send()
        for copy in near_out(d, low) + relay_out(d, low):
            copy.wait_send()
    for copy in pack_out:
        copy.wait_send()
    for t in range(stages):
        kv_copy(t).wait_send()


def relay_scratch(n):
    bf16, f32 = jnp.bfloat16, jnp.float32
    dma = pltpu.SemaphoreType.DMA
    half, doubles = n // 2, n // 4
    block = (TOK, HEADS, HD)

    def blocks(*lead):
        return pltpu.VMEM(lead + block, bf16)

    def lanes(*lead):
        return pltpu.VMEM(lead + (1, HD), f32)

    results = 3 * half + doubles
    return [
        pltpu.VMEM((PER_DEV, HEADS * HD), bf16), blocks(REQUESTS),
        blocks(half, CAP), blocks(half), blocks(doubles), blocks(half, CAP), blocks(half), blocks(doubles), blocks(half), blocks(half),
        blocks(half, CAP), blocks(half), blocks(half), blocks(half), blocks(doubles), blocks(results),
        lanes(half, CAP), lanes(half), lanes(half), lanes(half), lanes(doubles), lanes(results),
        pltpu.VMEM((n, 2, PER_DEV, HD), bf16),
        pltpu.VMEM((CAP * REGION, HD), bf16), pltpu.VMEM((CAP * REGION, HD), bf16),
        pltpu.VMEM((REQUESTS, TOK, HEADS, HD), f32), pltpu.VMEM((REQUESTS, HD), f32),
        blocks(REQUESTS), pltpu.VMEM((REQUESTS, HD), f32),
    ] + [pltpu.SMEM((size,), jnp.int32) for size in (n, n, n, 2 * doubles, 2 * doubles, REQUESTS)
    ] + [dma((half,))] * 18 + [dma((1,))] * 6 + [dma((int(math.log2(n)),))] * 2 + [dma((5,))]


def direct_scratch(n, hit_count):
    bf16, f32 = jnp.bfloat16, jnp.float32
    dma = pltpu.SemaphoreType.DMA
    block = (n, CAP, TOK, HEADS, HD)
    return [
        pltpu.VMEM((PER_DEV, HEADS * HD), bf16), pltpu.VMEM((REQUESTS, TOK, HEADS, HD), bf16),
        pltpu.VMEM(block, bf16), pltpu.VMEM(block, bf16),
        pltpu.VMEM(block, bf16), pltpu.VMEM(block, bf16),
        pltpu.VMEM((n, 1, HD), f32), pltpu.VMEM((n, 1, HD), f32),
        pltpu.VMEM((n, 2, PER_DEV, HD), bf16),
        pltpu.VMEM((CAP * REGION, HD), bf16), pltpu.VMEM((CAP * REGION, HD), bf16),
        pltpu.VMEM((REQUESTS, TOK, HEADS, HD), f32), pltpu.VMEM((REQUESTS, HD), f32),
        pltpu.VMEM((hit_count, REQUESTS, TOK, HEADS, HD), bf16),
        pltpu.VMEM((hit_count, REQUESTS, HD), f32),
    ] + [dma((n,))] * 6 + [dma((int(math.log2(n)),))] * 2 + [dma((5,))]


def solution(mesh):
    n = mesh.shape["cache"]

    def body(prefix_len, hits, span_block, queries, fresh_keys, fresh_values, cache_keys, cache_values):
        hit_count = hits.shape[1]
        vmem = pl.BlockSpec(memory_space=pltpu.VMEM)
        smem = pl.BlockSpec(memory_space=pltpu.SMEM)
        hbm = pl.BlockSpec(memory_space=pltpu.HBM)
        if hit_count == 1 and n // 2 == CAP * PLANE:
            program, scratch = functools.partial(relay_kernel, n), relay_scratch(n)
        else:
            program, scratch = functools.partial(kernel, n, hit_count), direct_scratch(n, hit_count)
        result = pl.pallas_call(
            program,
            out_shape=jax.ShapeDtypeStruct((PER_DEV, HEADS, HD), jnp.bfloat16),
            in_specs=[smem, smem, vmem, hbm, hbm, hbm, hbm, hbm],
            out_specs=vmem,
            scratch_shapes=scratch,
            compiler_params=pltpu.CompilerParams(
                collective_id=0, has_side_effects=True, vmem_limit_bytes=60 << 20),
        )(prefix_len, hits.reshape(-1), span_block, queries, fresh_keys, fresh_values, cache_keys, cache_values)
        return result.reshape(PER_DEV, HEADS * HD)

    in_specs = (
        P("groups"), P("groups", None), P("groups", None),
        P(("groups", "cache"), None), P(("groups", "cache"), None), P(("groups", "cache"), None),
        P(("groups", "cache"), None), P(("groups", "cache"), None),
    )
    return jax.shard_map(body, mesh=mesh, in_specs=in_specs,
                         out_specs=P(("groups", "cache"), None), check_vma=False)
```

```python
import functools
import math

import jax
import jax.numpy as jnp
from jax import lax
from jax.experimental import pallas as pl
from jax.experimental.pallas import tpu as pltpu
from jax.sharding import PartitionSpec as P

HEADS = 16
HD = 128
PAGE = 128
CAP = 2
REQUESTS = 16
TOK = 4
PAGES_DEV = 16
REGION = PAGES_DEV // CAP * PAGE
PER_DEV = REQUESTS * TOK
PLANE = 4
ROWS = PLANE * TOK * HEADS
MESH = pl.DeviceIdType.MESH
FLOOR = -1e30
EXP2_SCALE = HD**-0.5 * math.log2(math.e)


def flip(a, b, size):
    out, bit = 0, 1
    while bit < size:
        out = out + ((a // bit + b // bit) % 2) * bit
        bit *= 2
    return out


def attend(q, k, v, visible):
    s = lax.dot_general(q, k, (((1,), (1,)), ((), ())), preferred_element_type=jnp.float32)
    s = jnp.where(visible, s, FLOOR)
    m = jnp.max(s, axis=1, keepdims=True)
    p = jnp.exp2((s - m) * EXP2_SCALE).astype(jnp.bfloat16)
    v1 = jnp.concatenate([v, jnp.ones_like(v)], axis=1)
    o = jnp.dot(p, v1, preferred_element_type=jnp.float32)
    return m, o


def head_lanes(x, units, first):
    row = lax.broadcasted_iota(jnp.int32, (units, TOK * HEADS, HD), 1)
    lane = lax.broadcasted_iota(jnp.int32, (units, TOK * HEADS, HD), 2)
    wide = x.reshape(units, TOK * HEADS, HD)
    return jnp.sum(jnp.where(row + first == lane, wide, 0.0), axis=1)


def head_rows(x, units):
    row = lax.broadcasted_iota(jnp.int32, (units, TOK * HEADS, HD), 1)
    lane = lax.broadcasted_iota(jnp.int32, (units, TOK * HEADS, HD), 2)
    wide = jnp.broadcast_to(x[:, None, :], (units, TOK * HEADS, HD))
    return jnp.sum(jnp.where(row == lane, wide, 0.0), axis=2, keepdims=True)


def mirrored(a, size):
    out, bit = 0, 1
    while bit < size:
        out = out + ((a // bit) % 2) * (size // (2 * bit))
        bit *= 2
    return out


def kernel(n, hit_count, prefix, hits, span, queries, fk, fv, ck, cv, out,
           qin, qx, send, arrived, ret, back, lret, lback, kv, kc, vc, pout, plse, comb, lcomb,
           qs, qr, rs, rr, ls, lr, s1s, s1r, loc):
    me = lax.axis_index("cache")
    planes = n // PLANE
    stages = int(math.log2(n))
    spot_me = mirrored(me, n)
    my_plane = me // PLANE

    loads = [
        pltpu.make_async_copy(queries, qin, loc.at[4]),
        pltpu.make_async_copy(fk, kv.at[spot_me, 0], loc.at[0]),
        pltpu.make_async_copy(fv, kv.at[spot_me, 1], loc.at[1]),
        pltpu.make_async_copy(ck, kc, loc.at[2]),
        pltpu.make_async_copy(cv, vc, loc.at[3]),
    ]
    for load in loads:
        load.start()

    barrier = pltpu.get_barrier_semaphore()

    @pl.loop(1, n)
    def _(k):
        pl.semaphore_signal(barrier, inc=1, device_id={"cache": (me + k) % n}, device_id_type=MESH)

    def named_by(d):
        first = jnp.int32(REQUESTS - 1)
        last = jnp.int32(0)
        for r in range(REQUESTS):
            for i in range(hit_count):
                here = hits[r * hit_count + i] == d
                first = jnp.where(here, jnp.minimum(first, r), first)
                last = jnp.where(here, r, last)
        return first, last

    loads[0].wait()
    qx[...] = qin[...].reshape(REQUESTS, TOK, HEADS, HD)

    @pl.loop(0, n)
    def _(d):
        first, last = named_by(d)
        send[d, 0] = qx[first]
        send[d, 1] = qx[last]

    pl.semaphore_wait(barrier, n - 1)
    loads[1].wait()
    loads[2].wait()

    def kv_copy(t, mine=True):
        size = 2**t
        start = (spot_me // size) * size
        if not mine:
            start = flip(spot_me // size, 1, n // size) * size
        block = kv.at[pl.ds(start, size)]
        return pltpu.make_async_remote_copy(
            src_ref=block, dst_ref=block, send_sem=s1s.at[t], recv_sem=s1r.at[t],
            device_id={"cache": flip(me, n // (2 * size), n)}, device_id_type=MESH)

    kv_copy(0).start()

    def query_copy(to, frm):
        return pltpu.make_async_remote_copy(
            src_ref=send.at[to], dst_ref=arrived.at[frm], send_sem=qs.at[to], recv_sem=qr.at[frm],
            device_id={"cache": to}, device_id_type=MESH)

    def out_copy(to, frm):
        return pltpu.make_async_remote_copy(
            src_ref=ret.at[to], dst_ref=back.at[frm], send_sem=rs.at[to], recv_sem=rr.at[frm],
            device_id={"cache": to}, device_id_type=MESH)

    def lse_copy(to, frm):
        return pltpu.make_async_remote_copy(
            src_ref=lret.at[to], dst_ref=lback.at[frm], send_sem=ls.at[to], recv_sem=lr.at[frm],
            device_id={"cache": to}, device_id_type=MESH)

    def peers(j, act):
        base = flip(my_plane, j, planes) * PLANE

        @pl.loop(0, PLANE)
        def _(k):
            d = base + (me + k) % PLANE

            @pl.when(d != me)
            def _():
                act(d)

    @pl.loop(0, planes)
    def _(i):
        peers((i + 1) % planes, lambda d: query_copy(d, me).start())

    arrived[me] = send[me]
    loads[3].wait()
    loads[4].wait()

    limits = []
    for request in named_by(me):
        place = jnp.int32(0)
        for i in range(hit_count):
            place = jnp.where(hits[request * hit_count + i] == me, i, place)
        limits.append(prefix[request] - place * REGION)
    spot = lax.broadcasted_iota(jnp.int32, (1, REGION), 1)

    def serve(j):
        peers(j, lambda d: query_copy(d, d).wait_recv())
        base = flip(my_plane, j, planes) * PLANE
        lanes = jnp.zeros((PLANE, HD), jnp.float32)

        for slot in range(CAP):
            q = arrived[pl.ds(base, PLANE), slot].reshape(ROWS, HD)
            part = pl.ds(slot * REGION, REGION)
            m, o = attend(q, kc[part], vc[part], spot < limits[slot])
            total = jnp.maximum(o[:, HD:], 1.0)
            lse = m * EXP2_SCALE + jnp.log2(total)
            lse = jnp.where(limits[slot] > 0, lse, FLOOR)
            result = (o[:, :HD] / total).astype(jnp.bfloat16)
            ret[pl.ds(base, PLANE), slot] = result.reshape(PLANE, TOK, HEADS, HD)
            lanes = lanes + head_lanes(lse, PLANE, slot * TOK * HEADS)
        for k in range(PLANE):
            lret[base + k] = lanes[k:k + 1]

        def go(d):
            out_copy(d, me).start()
            lse_copy(d, me).start()

        peers(j, go)

        for t in range(stages - 1):
            @pl.when(j == t)
            def _():
                kv_copy(t, mine=False).wait_recv()
                kv_copy(t + 1).start()

    pl.loop(0, planes)(serve)
    back[me] = ret[me]
    lback[me] = lret[me]
    kv_copy(stages - 1, mine=False).wait_recv()

    span_f = span[...].astype(jnp.float32)
    mine = jnp.sum(
        jnp.where(lax.broadcasted_iota(jnp.int32, span_f.shape, 1) == me, span_f, 0.0),
        axis=1, keepdims=True)
    order = jnp.clip(span_f - mine, -1.0, 1.0).astype(jnp.bfloat16)
    group = 16
    keys = group * PER_DEV
    chunks = n // group
    key_lane = lax.broadcasted_iota(jnp.int32, (REQUESTS, keys), 1)
    key_row = lax.broadcasted_iota(jnp.int32, (REQUESTS, keys), 0)

    def ranks(chunk):
        lane = lax.broadcasted_iota(jnp.int32, (n, keys), 1)
        dev = lax.broadcasted_iota(jnp.int32, (n, keys), 0)
        pick = jnp.where(mirrored(lane // PER_DEV + chunk * group, n) == dev, 1.0, 0.0).astype(jnp.bfloat16)
        step = jnp.dot(order, pick, preferred_element_type=jnp.float32)
        spot_rank = step * TOK + (key_lane % TOK).astype(jnp.float32)
        same = (key_lane // TOK) % REQUESTS == key_row
        return jnp.where(same, spot_rank, 100.0).astype(jnp.bfloat16)

    def kv_rows(chunk, which):
        return kv[pl.ds(chunk * group, group), which].reshape(keys, HD)

    def prompt_part(c, chunk, rank):
        q = qx_rows(c)
        row = lax.broadcasted_iota(jnp.int32, (ROWS, REQUESTS), 0)
        req = lax.broadcasted_iota(jnp.int32, (ROWS, REQUESTS), 1)
        spread = jnp.where(row // (TOK * HEADS) + c * (ROWS // (TOK * HEADS)) == req, 1.0, 0.0)
        ranked = jnp.dot(spread.astype(jnp.bfloat16), rank, preferred_element_type=jnp.float32)
        token = (lax.broadcasted_iota(jnp.int32, (ROWS, 1), 0) // HEADS) % TOK
        return attend(q, kv_rows(chunk, 0), kv_rows(chunk, 1), ranked <= token.astype(jnp.float32))

    reqs = ROWS // (TOK * HEADS)

    def qx_rows(c):
        return qx[pl.ds(c * reqs, reqs)].reshape(ROWS, HD)

    rank0 = ranks(0) if chunks == 1 else None

    @pl.loop(0, REQUESTS // reqs)
    def _(c):
        if chunks == 1:
            m, o = prompt_part(c, 0, rank0)
        else:
            def more(chunk, carry):
                m0, o0 = carry
                m1, o1 = prompt_part(c, chunk, ranks(chunk))
                m2 = jnp.maximum(m0, m1)
                return m2, (o0 * jnp.exp2((m0 - m2) * EXP2_SCALE)
                            + o1 * jnp.exp2((m1 - m2) * EXP2_SCALE))
            m, o = lax.fori_loop(0, chunks, more, (
                jnp.full((ROWS, 1), FLOOR, jnp.float32), jnp.zeros((ROWS, 2 * HD), jnp.float32)))
        total = o[:, HD:]
        pout[pl.ds(c * reqs, reqs)] = (o[:, :HD] / total).reshape(reqs, TOK, HEADS, HD)
        plse[pl.ds(pl.multiple_of(c * reqs, reqs), reqs)] = head_lanes(m * EXP2_SCALE + jnp.log2(total), reqs, 0)

    def finish(d):
        out_copy(d, d).wait_recv()
        lse_copy(d, d).wait_recv()

    pl.loop(0, planes)(lambda j: peers(j, finish))

    for i in range(hit_count):
        for r in range(REQUESTS):
            owner = hits[r * hit_count + i]
            rank = jnp.int32(0)
            for r2 in range(r):
                for i2 in range(hit_count):
                    rank = jnp.where(hits[r2 * hit_count + i2] == owner, rank + 1, rank)
            rank = jnp.minimum(rank, CAP - 1)
            comb[i, r] = back[owner, rank]
            row = lback[owner]
            lcomb[i, r:r + 1] = jnp.where(rank == 0, row, pltpu.roll(row, HD // 2, 1))

    top = plse[...]
    for i in range(hit_count):
        top = jnp.maximum(top, lcomb[i])
    share = jnp.exp2(plse[...] - top)
    shares = [jnp.exp2(lcomb[i] - top) for i in range(hit_count)]
    scale = 1.0 / functools.reduce(jnp.add, shares, share)
    whole = (REQUESTS, TOK * HEADS, HD)
    mixed = head_rows(share * scale, REQUESTS) * pout[...].reshape(whole)
    for i in range(hit_count):
        mixed = mixed + head_rows(shares[i] * scale, REQUESTS) * comb[i].reshape(whole).astype(jnp.float32)
    out[...] = mixed.astype(jnp.bfloat16).reshape(PER_DEV, HEADS, HD)

    def drained(d):
        query_copy(d, me).wait_send()
        out_copy(d, me).wait_send()
        lse_copy(d, me).wait_send()

    pl.loop(0, planes)(lambda j: peers(j, drained))
    for t in range(stages):
        kv_copy(t).wait_send()


def toggle(a, mask):
    out, bit = a, 1
    while bit <= mask:
        if mask & bit:
            out = out + bit - 2 * bit * ((a // bit) % 2)
        bit *= 2
    return out


def relay_kernel(n, prefix, hits, span, queries, fk, fv, ck, cv, out,
                 qin, qx, near_s, far_s, pack_s, near_in, far_in, pack_in, fwd, rel_in,
                 near_o, far_o, rel_o, relr, packr, back, near_l, far_l, rel_l, relr_l, packr_l, lback,
                 kv, kc, vc, pout, plse, comb, lcomb, firsts, lasts, doubled, chosen, owners, places,
                 nqs, nqr, fqs, fqr, wqs, wqr, nrs, nrr, frs, frr, wrs, wrr,
                 nls, nlr, fls, flr, wls, wlr, pqs, pqr, prs, prr, pls, plr, s1s, s1r, loc):
    me = lax.axis_index("cache")
    half = n // 2
    doubles = n // 4
    low = me % half
    side = me // half
    other = toggle(me, half)
    stages = int(math.log2(n))
    spot_me = mirrored(me, n)
    my_plane = (low // PLANE) * PLANE
    near_far = 2 * half
    packed = 3 * half

    loads = [
        pltpu.make_async_copy(queries, qin, loc.at[4]),
        pltpu.make_async_copy(fk, kv.at[spot_me, 0], loc.at[0]),
        pltpu.make_async_copy(fv, kv.at[spot_me, 1], loc.at[1]),
        pltpu.make_async_copy(ck, kc, loc.at[2]),
        pltpu.make_async_copy(cv, vc, loc.at[3]),
    ]
    for load in loads:
        load.start()

    barrier = pltpu.get_barrier_semaphore()
    for mask in reversed(range(1, n)):
        pl.semaphore_signal(barrier, inc=1, device_id={"cache": toggle(me, mask)}, device_id_type=MESH)

    for part in range(2):
        seen = jnp.int32(0)
        picks = [jnp.int32(0)] * doubles
        lows = [jnp.int32(0)] * doubles
        for spot in range(half):
            d = part * half + spot
            first = jnp.int32(REQUESTS - 1)
            last = jnp.int32(0)
            for r in reversed(range(REQUESTS)):
                first = jnp.where(hits[r] == d, r, first)
            for r in range(REQUESTS):
                last = jnp.where(hits[r] == d, r, last)
            firsts[d] = first
            lasts[d] = last
            doubled[d] = jnp.minimum(seen, doubles - 1)
            two = first < last
            for j in range(doubles):
                here = two & (seen == j)
                picks[j] = jnp.where(here, last, picks[j])
                lows[j] = jnp.where(here, spot, lows[j])
            seen = jnp.where(two, seen + 1, seen)
        for j in range(doubles):
            chosen[part * doubles + j] = picks[j]
            owners[part * doubles + j] = lows[j]

    for r in range(REQUESTS):
        owner = hits[r]
        second = firsts[owner] < r
        at_low = owner % half
        inside = 2 * at_low + jnp.where(second, 1, 0)
        outside = jnp.where(second, packed + doubled[owner], near_far + at_low)
        places[r] = jnp.where(owner // half == side, inside, outside)

    loads[0].wait()
    qx[...] = qin[...].reshape(REQUESTS, TOK, HEADS, HD)
    for j in range(doubles):
        pack_s[j] = qx[chosen[(1 - side) * doubles + j]]

    @pl.loop(0, half)
    def _(d):
        near_s[d, 0] = qx[firsts[side * half + d]]
        near_s[d, 1] = qx[lasts[side * half + d]]
        far_s[d] = qx[firsts[(1 - side) * half + d]]

    near_in[low] = near_s[low]
    for load in loads[1:]:
        load.wait()
    pl.semaphore_wait(barrier, n - 1)

    def remote(src, dst, sent, got, to):
        return pltpu.make_async_remote_copy(
            src_ref=src, dst_ref=dst, send_sem=sent, recv_sem=got,
            device_id={"cache": to}, device_id_type=MESH)

    def kv_copy(t, mine=True):
        size = 2**t
        start = (spot_me // size) * size
        if not mine:
            start = flip(spot_me // size, 1, n // size) * size
        block = kv.at[pl.ds(start, size)]
        return remote(block, block, s1s.at[t], s1r.at[t], toggle(me, n // (2 * size)))

    def inner(d):
        return side * half + d

    def outer(d):
        return (1 - side) * half + d

    def near_query(to, frm):
        return remote(near_s.at[to], near_in.at[frm], nqs.at[to], nqr.at[frm], inner(to))

    def far_query(to, frm):
        return remote(far_s.at[to], far_in.at[frm], fqs.at[to], fqr.at[frm], outer(to))

    def relay_query(to, frm):
        return remote(fwd.at[to], rel_in.at[frm], wqs.at[to], wqr.at[frm], inner(to))

    def near_out(to, frm):
        return (remote(near_o.at[to], back.at[pl.ds(2 * frm, 2)], nrs.at[to], nrr.at[frm], inner(to)),
                remote(near_l.at[to], lback.at[pl.ds(2 * frm, 2)], nls.at[to], nlr.at[frm], inner(to)))

    def far_out(to, frm):
        return (remote(far_o.at[to], back.at[near_far + frm], frs.at[to], frr.at[frm], outer(to)),
                remote(far_l.at[to], lback.at[near_far + frm], fls.at[to], flr.at[frm], outer(to)))

    def relay_out(to, frm):
        return (remote(rel_o.at[to], relr.at[frm], wrs.at[to], wrr.at[frm], inner(to)),
                remote(rel_l.at[to], relr_l.at[frm], wls.at[to], wlr.at[frm], inner(to)))

    pack_query = remote(pack_s, pack_in, pqs.at[0], pqr.at[0], other)
    pack_out = (remote(packr, back.at[pl.ds(packed, doubles)], prs.at[0], prr.at[0], other),
                remote(packr_l, lback.at[pl.ds(packed, doubles)], pls.at[0], plr.at[0], other))

    near_masks = list(range(1, half))
    plane_masks = list(range(1, PLANE))
    cross_masks = list(range(PLANE, half))

    limits = [prefix[firsts[me]], prefix[lasts[me]]]
    spot = lax.broadcasted_iota(jnp.int32, (1, REGION), 1)

    def answer(q, slot):
        part = pl.ds(slot * REGION, REGION)
        m, o = attend(q.reshape(ROWS, HD), kc[part], vc[part], spot < limits[slot])
        total = jnp.maximum(o[:, HD:], 1.0)
        lse = m * EXP2_SCALE + jnp.log2(total)
        result = (o[:, :HD] / total).astype(jnp.bfloat16)
        return result.reshape(PLANE, TOK, HEADS, HD), head_lanes(lse, PLANE, 0)

    def near_group(base, masks):
        for mask in masks:
            d = toggle(low, mask)
            near_query(d, d).wait_recv()
        group = pl.ds(base, PLANE)
        for slot in range(CAP):
            result, lanes = answer(near_in[group, slot], slot)
            near_o[group, slot] = result
            for k in range(PLANE):
                near_l[base + k, slot] = lanes[k:k + 1]

    def near_reply(masks):
        for mask in masks:
            for copy in near_out(toggle(low, mask), low):
                copy.start()

    def far_group(base, masks):
        for mask in masks:
            d = toggle(low, mask)
            far_query(d, d).wait_recv()
        group = pl.ds(base, PLANE)
        result, lanes = answer(far_in[group], 0)
        far_o[group] = result
        for k in range(PLANE):
            far_l[base + k] = lanes[k:k + 1]
        for mask in masks:
            for copy in far_out(toggle(low, mask), low):
                copy.start()

    def relay_group(base, masks):
        for mask in masks:
            d = toggle(low, mask)
            relay_query(d, d).wait_recv()
        group = pl.ds(base, PLANE)
        result, lanes = answer(rel_in[group], 1)
        rel_o[group] = result
        for k in range(PLANE):
            rel_l[base + k] = lanes[k:k + 1]
        for mask in masks:
            for copy in relay_out(toggle(low, mask), low):
                copy.start()

    def next_kv(t):
        kv_copy(t, mine=False).wait_recv()
        kv_copy(t + 1).start()

    plane_next = toggle(low, PLANE) // PLANE * PLANE

    def far_start(masks):
        for mask in masks:
            far_query(toggle(low, mask), low).start()

    def near_start(masks):
        for mask in masks:
            near_query(toggle(low, mask), low).start()

    def forward():
        pack_query.wait_recv()

        @pl.loop(0, half)
        def _(d):
            fwd[d] = pack_in[doubled[side * half + d]]

        rel_in[low] = fwd[low]
        for mask in cross_masks + plane_masks:
            relay_query(toggle(low, mask), low).start()

    def gather_results():
        for mask in near_masks:
            d = toggle(low, mask)
            for copy in relay_out(d, d):
                copy.wait_recv()
        for j in range(doubles):
            packr[j] = relr[owners[side * doubles + j]]
            packr_l[j] = relr_l[owners[side * doubles + j]]
        for copy in pack_out:
            copy.start()

    def prompt():
        span_f = span[...].astype(jnp.float32)
        mine = jnp.sum(
            jnp.where(lax.broadcasted_iota(jnp.int32, span_f.shape, 1) == me, span_f, 0.0),
            axis=1, keepdims=True)
        order = jnp.clip(span_f - mine, -1.0, 1.0).astype(jnp.bfloat16)
        reqs = ROWS // (TOK * HEADS)
        rows = reqs * TOK
        keys = n * rows
        key_lane = lax.broadcasted_iota(jnp.int32, (REQUESTS, keys), 1)
        key_row = lax.broadcasted_iota(jnp.int32, (REQUESTS, keys), 0)
        lane = lax.broadcasted_iota(jnp.int32, (n, keys), 1)
        dev = lax.broadcasted_iota(jnp.int32, (n, keys), 0)
        pick = jnp.where(mirrored(lane // rows, n) == dev, 1.0, 0.0).astype(jnp.bfloat16)
        step = jnp.dot(order, pick, preferred_element_type=jnp.float32)
        rank_all = step * TOK + (key_lane % TOK).astype(jnp.float32)
        token = ((lax.broadcasted_iota(jnp.int32, (ROWS, 1), 0) // HEADS) % TOK).astype(jnp.float32)
        row_at = lax.broadcasted_iota(jnp.int32, (ROWS, REQUESTS), 0) // (TOK * HEADS)
        req_at = lax.broadcasted_iota(jnp.int32, (ROWS, REQUESTS), 1)

        @pl.loop(0, REQUESTS // reqs)
        def _(c):
            same = (key_lane // TOK) % reqs + c * reqs == key_row
            rank = jnp.where(same, rank_all, 100.0).astype(jnp.bfloat16)
            spread = jnp.where(row_at + c * reqs == req_at, 1.0, 0.0).astype(jnp.bfloat16)
            ranked = jnp.dot(spread, rank, preferred_element_type=jnp.float32)
            part = pl.ds(pl.multiple_of(c * rows, rows), rows)
            m, o = attend(qx[pl.ds(c * reqs, reqs)].reshape(ROWS, HD), kv[:, 0, part].reshape(keys, HD),
                          kv[:, 1, part].reshape(keys, HD), ranked <= token)
            total = o[:, HD:]
            pout[pl.ds(pl.multiple_of(c * ROWS, ROWS), ROWS)] = o[:, :HD] / total
            plse[pl.ds(pl.multiple_of(c * reqs, reqs), reqs)] = head_lanes(m * EXP2_SCALE + jnp.log2(total), reqs, 0)


    near_start(plane_masks)
    kv_copy(0).start()
    near_start(cross_masks)
    pack_query.start()
    far_start([0] + plane_masks)
    near_group(my_plane, plane_masks)
    back[pl.ds(2 * low, 2)] = near_o[low]
    lback[pl.ds(2 * low, 2)] = near_l[low]
    near_reply(plane_masks)
    next_kv(0)
    forward()
    far_start(cross_masks)
    near_group(plane_next, cross_masks)
    next_kv(1)
    near_reply(cross_masks)
    far_group(my_plane, [0] + plane_masks)
    relay_group(my_plane, plane_masks)
    relr[low] = rel_o[low]
    relr_l[low] = rel_l[low]
    relay_group(plane_next, cross_masks)
    far_group(plane_next, cross_masks)
    gather_results()
    next_kv(2)
    kv_copy(stages - 1, mine=False).wait_recv()
    prompt()

    for mask in near_masks:
        d = toggle(low, mask)
        for copy in near_out(d, d):
            copy.wait_recv()
    for mask in range(half):
        d = toggle(low, mask)
        for copy in far_out(d, d):
            copy.wait_recv()
    for copy in pack_out:
        copy.wait_recv()

    for r in range(REQUESTS):
        comb[r] = back[places[r]]
        lcomb[r:r + 1] = lback[places[r]]
    top = jnp.maximum(plse[...], lcomb[...])
    share = jnp.exp2(plse[...] - top)
    taken = jnp.exp2(lcomb[...] - top)
    scale = 1.0 / (share + taken)
    whole = (REQUESTS, TOK * HEADS, HD)
    mixed = head_rows(share * scale, REQUESTS) * pout[...].reshape(whole)
    mixed = mixed + head_rows(taken * scale, REQUESTS) * comb[...].reshape(whole).astype(jnp.float32)
    pout[...] = mixed.reshape(PER_DEV * HEADS, HD)
    for h in range(HEADS):
        out[:, h * HD:(h + 1) * HD] = pout[pl.ds(h, PER_DEV, stride=HEADS)].astype(jnp.bfloat16)

    pack_query.wait_send()
    for mask in [0] + plane_masks:
        far_query(toggle(low, mask), low).wait_send()
    for mask in cross_masks:
        near_query(toggle(low, mask), low).wait_send()
    for mask in cross_masks:
        far_query(toggle(low, mask), low).wait_send()
    for mask in plane_masks:
        near_query(toggle(low, mask), low).wait_send()
    for mask in range(half):
        for copy in far_out(toggle(low, mask), low):
            copy.wait_send()
    for mask in near_masks:
        d = toggle(low, mask)
        relay_query(d, low).wait_send()
        for copy in near_out(d, low) + relay_out(d, low):
            copy.wait_send()
    for copy in pack_out:
        copy.wait_send()
    for t in range(0, stages):
        kv_copy(t).wait_send()


def relay_scratch(n):
    bf16, f32 = jnp.bfloat16, jnp.float32
    dma = pltpu.SemaphoreType.DMA
    half, doubles = n // 2, n // 4
    block = (TOK, HEADS, HD)

    def blocks(*lead):
        return pltpu.VMEM(lead + block, bf16)

    def lanes(*lead):
        return pltpu.VMEM(lead + (1, HD), f32)

    results = 3 * half + doubles
    return [
        pltpu.VMEM((PER_DEV, HEADS * HD), bf16), blocks(REQUESTS),
        blocks(half, CAP), blocks(half), blocks(doubles), blocks(half, CAP), blocks(half), blocks(doubles), blocks(half), blocks(half),
        blocks(half, CAP), blocks(half), blocks(half), blocks(half), blocks(doubles), blocks(results),
        lanes(half, CAP), lanes(half), lanes(half), lanes(half), lanes(doubles), lanes(results),
        pltpu.VMEM((n, 2, PER_DEV, HD), bf16),
        pltpu.VMEM((CAP * REGION, HD), bf16), pltpu.VMEM((CAP * REGION, HD), bf16),
        pltpu.VMEM((PER_DEV * HEADS, HD), f32), pltpu.VMEM((REQUESTS, HD), f32),
        blocks(REQUESTS), pltpu.VMEM((REQUESTS, HD), f32),
    ] + [pltpu.SMEM((size,), jnp.int32) for size in (n, n, n, 2 * doubles, 2 * doubles, REQUESTS)
    ] + [dma((half,))] * 18 + [dma((1,))] * 6 + [dma((int(math.log2(n)),))] * 2 + [dma((5,))]


def direct_scratch(n, hit_count):
    bf16, f32 = jnp.bfloat16, jnp.float32
    dma = pltpu.SemaphoreType.DMA
    block = (n, CAP, TOK, HEADS, HD)
    return [
        pltpu.VMEM((PER_DEV, HEADS * HD), bf16), pltpu.VMEM((REQUESTS, TOK, HEADS, HD), bf16),
        pltpu.VMEM(block, bf16), pltpu.VMEM(block, bf16),
        pltpu.VMEM(block, bf16), pltpu.VMEM(block, bf16),
        pltpu.VMEM((n, 1, HD), f32), pltpu.VMEM((n, 1, HD), f32),
        pltpu.VMEM((n, 2, PER_DEV, HD), bf16),
        pltpu.VMEM((CAP * REGION, HD), bf16), pltpu.VMEM((CAP * REGION, HD), bf16),
        pltpu.VMEM((REQUESTS, TOK, HEADS, HD), f32), pltpu.VMEM((REQUESTS, HD), f32),
        pltpu.VMEM((hit_count, REQUESTS, TOK, HEADS, HD), bf16),
        pltpu.VMEM((hit_count, REQUESTS, HD), f32),
    ] + [dma((n,))] * 6 + [dma((int(math.log2(n)),))] * 2 + [dma((5,))]


def solution(mesh):
    n = mesh.shape["cache"]

    def body(prefix_len, hits, span_block, queries, fresh_keys, fresh_values, cache_keys, cache_values):
        hit_count = hits.shape[1]
        vmem = pl.BlockSpec(memory_space=pltpu.VMEM)
        smem = pl.BlockSpec(memory_space=pltpu.SMEM)
        hbm = pl.BlockSpec(memory_space=pltpu.HBM)
        if hit_count == 1 and n // 2 == CAP * PLANE:
            program, scratch, shape = functools.partial(relay_kernel, n), relay_scratch(n), (PER_DEV, HEADS * HD)
        else:
            program, scratch = functools.partial(kernel, n, hit_count), direct_scratch(n, hit_count)
            shape = (PER_DEV, HEADS, HD)
        result = pl.pallas_call(
            program,
            out_shape=pltpu.VMEM(shape, jnp.bfloat16),
            in_specs=[smem, smem, vmem, hbm, hbm, hbm, hbm, hbm],
            out_specs=vmem,
            scratch_shapes=scratch,
            compiler_params=pltpu.CompilerParams(
                collective_id=0, has_side_effects=True, vmem_limit_bytes=60 << 20),
        )(prefix_len, hits.reshape(-1), span_block, queries, fresh_keys, fresh_values, cache_keys, cache_values)
        return result.reshape(PER_DEV, HEADS * HD)

    in_specs = (
        P("groups"), P("groups", None), P("groups", None),
        P(("groups", "cache"), None), P(("groups", "cache"), None), P(("groups", "cache"), None),
        P(("groups", "cache"), None), P(("groups", "cache"), None),
    )
    return jax.shard_map(body, mesh=mesh, in_specs=in_specs,
                         out_specs=P(("groups", "cache"), None), check_vma=False)
```

```python
import functools
import math

import jax
import jax.numpy as jnp
from jax import lax
from jax.experimental import pallas as pl
from jax.experimental.pallas import tpu as pltpu
from jax.sharding import PartitionSpec as P

HEADS = 16
HD = 128
PAGE = 128
CAP = 2
REQUESTS = 16
TOK = 4
PAGES_DEV = 16
REGION = PAGES_DEV // CAP * PAGE
PER_DEV = REQUESTS * TOK
PLANE = 4
ROWS = PLANE * TOK * HEADS
MESH = pl.DeviceIdType.MESH
FLOOR = -1e30
EXP2_SCALE = HD**-0.5 * math.log2(math.e)


def flip(a, b, size):
    out, bit = 0, 1
    while bit < size:
        out = out + ((a // bit + b // bit) % 2) * bit
        bit *= 2
    return out


def attend(q, k, v, visible):
    s = lax.dot_general(q, k, (((1,), (1,)), ((), ())), preferred_element_type=jnp.float32)
    s = jnp.where(visible, s, FLOOR)
    m = jnp.max(s, axis=1, keepdims=True)
    p = jnp.exp2((s - m) * EXP2_SCALE).astype(jnp.bfloat16)
    v1 = jnp.concatenate([v, jnp.ones_like(v)], axis=1)
    o = jnp.dot(p, v1, preferred_element_type=jnp.float32)
    return m, o


def head_lanes(x, units, first):
    row = lax.broadcasted_iota(jnp.int32, (units, TOK * HEADS, HD), 1)
    lane = lax.broadcasted_iota(jnp.int32, (units, TOK * HEADS, HD), 2)
    wide = x.reshape(units, TOK * HEADS, HD)
    return jnp.sum(jnp.where(row + first == lane, wide, 0.0), axis=1)


def head_rows(x, units):
    row = lax.broadcasted_iota(jnp.int32, (units, TOK * HEADS, HD), 1)
    lane = lax.broadcasted_iota(jnp.int32, (units, TOK * HEADS, HD), 2)
    wide = jnp.broadcast_to(x[:, None, :], (units, TOK * HEADS, HD))
    return jnp.sum(jnp.where(row == lane, wide, 0.0), axis=2, keepdims=True)


def mirrored(a, size):
    out, bit = 0, 1
    while bit < size:
        out = out + ((a // bit) % 2) * (size // (2 * bit))
        bit *= 2
    return out


def kernel(n, hit_count, prefix, hits, span, queries, fk, fv, ck, cv, out,
           qin, qx, send, arrived, ret, back, lret, lback, kv, kc, vc, pout, plse, comb, lcomb,
           qs, qr, rs, rr, ls, lr, s1s, s1r, loc):
    me = lax.axis_index("cache")
    planes = n // PLANE
    stages = int(math.log2(n))
    spot_me = mirrored(me, n)
    my_plane = me // PLANE

    loads = [
        pltpu.make_async_copy(queries, qin, loc.at[4]),
        pltpu.make_async_copy(fk, kv.at[spot_me, 0], loc.at[0]),
        pltpu.make_async_copy(fv, kv.at[spot_me, 1], loc.at[1]),
        pltpu.make_async_copy(ck, kc, loc.at[2]),
        pltpu.make_async_copy(cv, vc, loc.at[3]),
    ]
    for load in loads:
        load.start()

    barrier = pltpu.get_barrier_semaphore()

    @pl.loop(1, n)
    def _(k):
        pl.semaphore_signal(barrier, inc=1, device_id={"cache": (me + k) % n}, device_id_type=MESH)

    def named_by(d):
        first = jnp.int32(REQUESTS - 1)
        last = jnp.int32(0)
        for r in range(REQUESTS):
            for i in range(hit_count):
                here = hits[r * hit_count + i] == d
                first = jnp.where(here, jnp.minimum(first, r), first)
                last = jnp.where(here, r, last)
        return first, last

    loads[0].wait()
    qx[...] = qin[...].reshape(REQUESTS, TOK, HEADS, HD)

    @pl.loop(0, n)
    def _(d):
        first, last = named_by(d)
        send[d, 0] = qx[first]
        send[d, 1] = qx[last]

    pl.semaphore_wait(barrier, n - 1)
    loads[1].wait()
    loads[2].wait()

    def kv_copy(t, mine=True):
        size = 2**t
        start = (spot_me // size) * size
        if not mine:
            start = flip(spot_me // size, 1, n // size) * size
        block = kv.at[pl.ds(start, size)]
        return pltpu.make_async_remote_copy(
            src_ref=block, dst_ref=block, send_sem=s1s.at[t], recv_sem=s1r.at[t],
            device_id={"cache": flip(me, n // (2 * size), n)}, device_id_type=MESH)

    kv_copy(0).start()

    def query_copy(to, frm):
        return pltpu.make_async_remote_copy(
            src_ref=send.at[to], dst_ref=arrived.at[frm], send_sem=qs.at[to], recv_sem=qr.at[frm],
            device_id={"cache": to}, device_id_type=MESH)

    def out_copy(to, frm):
        return pltpu.make_async_remote_copy(
            src_ref=ret.at[to], dst_ref=back.at[frm], send_sem=rs.at[to], recv_sem=rr.at[frm],
            device_id={"cache": to}, device_id_type=MESH)

    def lse_copy(to, frm):
        return pltpu.make_async_remote_copy(
            src_ref=lret.at[to], dst_ref=lback.at[frm], send_sem=ls.at[to], recv_sem=lr.at[frm],
            device_id={"cache": to}, device_id_type=MESH)

    def peers(j, act):
        base = flip(my_plane, j, planes) * PLANE

        @pl.loop(0, PLANE)
        def _(k):
            d = base + (me + k) % PLANE

            @pl.when(d != me)
            def _():
                act(d)

    @pl.loop(0, planes)
    def _(i):
        peers((i + 1) % planes, lambda d: query_copy(d, me).start())

    arrived[me] = send[me]
    loads[3].wait()
    loads[4].wait()

    limits = []
    for request in named_by(me):
        place = jnp.int32(0)
        for i in range(hit_count):
            place = jnp.where(hits[request * hit_count + i] == me, i, place)
        limits.append(prefix[request] - place * REGION)
    spot = lax.broadcasted_iota(jnp.int32, (1, REGION), 1)

    def serve(j):
        peers(j, lambda d: query_copy(d, d).wait_recv())
        base = flip(my_plane, j, planes) * PLANE
        lanes = jnp.zeros((PLANE, HD), jnp.float32)

        for slot in range(CAP):
            q = arrived[pl.ds(base, PLANE), slot].reshape(ROWS, HD)
            part = pl.ds(slot * REGION, REGION)
            m, o = attend(q, kc[part], vc[part], spot < limits[slot])
            total = jnp.maximum(o[:, HD:], 1.0)
            lse = m * EXP2_SCALE + jnp.log2(total)
            lse = jnp.where(limits[slot] > 0, lse, FLOOR)
            result = (o[:, :HD] / total).astype(jnp.bfloat16)
            ret[pl.ds(base, PLANE), slot] = result.reshape(PLANE, TOK, HEADS, HD)
            lanes = lanes + head_lanes(lse, PLANE, slot * TOK * HEADS)
        for k in range(PLANE):
            lret[base + k] = lanes[k:k + 1]

        def go(d):
            out_copy(d, me).start()
            lse_copy(d, me).start()

        peers(j, go)

        for t in range(stages - 1):
            @pl.when(j == t)
            def _():
                kv_copy(t, mine=False).wait_recv()
                kv_copy(t + 1).start()

    pl.loop(0, planes)(serve)
    back[me] = ret[me]
    lback[me] = lret[me]
    kv_copy(stages - 1, mine=False).wait_recv()

    span_f = span[...].astype(jnp.float32)
    mine = jnp.sum(
        jnp.where(lax.broadcasted_iota(jnp.int32, span_f.shape, 1) == me, span_f, 0.0),
        axis=1, keepdims=True)
    order = jnp.clip(span_f - mine, -1.0, 1.0).astype(jnp.bfloat16)
    group = 16
    keys = group * PER_DEV
    chunks = n // group
    key_lane = lax.broadcasted_iota(jnp.int32, (REQUESTS, keys), 1)
    key_row = lax.broadcasted_iota(jnp.int32, (REQUESTS, keys), 0)

    def ranks(chunk):
        lane = lax.broadcasted_iota(jnp.int32, (n, keys), 1)
        dev = lax.broadcasted_iota(jnp.int32, (n, keys), 0)
        pick = jnp.where(mirrored(lane // PER_DEV + chunk * group, n) == dev, 1.0, 0.0).astype(jnp.bfloat16)
        step = jnp.dot(order, pick, preferred_element_type=jnp.float32)
        spot_rank = step * TOK + (key_lane % TOK).astype(jnp.float32)
        same = (key_lane // TOK) % REQUESTS == key_row
        return jnp.where(same, spot_rank, 100.0).astype(jnp.bfloat16)

    def kv_rows(chunk, which):
        return kv[pl.ds(chunk * group, group), which].reshape(keys, HD)

    def prompt_part(c, chunk, rank):
        q = qx_rows(c)
        row = lax.broadcasted_iota(jnp.int32, (ROWS, REQUESTS), 0)
        req = lax.broadcasted_iota(jnp.int32, (ROWS, REQUESTS), 1)
        spread = jnp.where(row // (TOK * HEADS) + c * (ROWS // (TOK * HEADS)) == req, 1.0, 0.0)
        ranked = jnp.dot(spread.astype(jnp.bfloat16), rank, preferred_element_type=jnp.float32)
        token = (lax.broadcasted_iota(jnp.int32, (ROWS, 1), 0) // HEADS) % TOK
        return attend(q, kv_rows(chunk, 0), kv_rows(chunk, 1), ranked <= token.astype(jnp.float32))

    reqs = ROWS // (TOK * HEADS)

    def qx_rows(c):
        return qx[pl.ds(c * reqs, reqs)].reshape(ROWS, HD)

    rank0 = ranks(0) if chunks == 1 else None

    @pl.loop(0, REQUESTS // reqs)
    def _(c):
        if chunks == 1:
            m, o = prompt_part(c, 0, rank0)
        else:
            def more(chunk, carry):
                m0, o0 = carry
                m1, o1 = prompt_part(c, chunk, ranks(chunk))
                m2 = jnp.maximum(m0, m1)
                return m2, (o0 * jnp.exp2((m0 - m2) * EXP2_SCALE)
                            + o1 * jnp.exp2((m1 - m2) * EXP2_SCALE))
            m, o = lax.fori_loop(0, chunks, more, (
                jnp.full((ROWS, 1), FLOOR, jnp.float32), jnp.zeros((ROWS, 2 * HD), jnp.float32)))
        total = o[:, HD:]
        pout[pl.ds(c * reqs, reqs)] = (o[:, :HD] / total).reshape(reqs, TOK, HEADS, HD)
        plse[pl.ds(pl.multiple_of(c * reqs, reqs), reqs)] = head_lanes(m * EXP2_SCALE + jnp.log2(total), reqs, 0)

    def finish(d):
        out_copy(d, d).wait_recv()
        lse_copy(d, d).wait_recv()

    pl.loop(0, planes)(lambda j: peers(j, finish))

    for i in range(hit_count):
        for r in range(REQUESTS):
            owner = hits[r * hit_count + i]
            rank = jnp.int32(0)
            for r2 in range(r):
                for i2 in range(hit_count):
                    rank = jnp.where(hits[r2 * hit_count + i2] == owner, rank + 1, rank)
            rank = jnp.minimum(rank, CAP - 1)
            comb[i, r] = back[owner, rank]
            row = lback[owner]
            lcomb[i, r:r + 1] = jnp.where(rank == 0, row, pltpu.roll(row, HD // 2, 1))

    top = plse[...]
    for i in range(hit_count):
        top = jnp.maximum(top, lcomb[i])
    share = jnp.exp2(plse[...] - top)
    shares = [jnp.exp2(lcomb[i] - top) for i in range(hit_count)]
    scale = 1.0 / functools.reduce(jnp.add, shares, share)
    whole = (REQUESTS, TOK * HEADS, HD)
    mixed = head_rows(share * scale, REQUESTS) * pout[...].reshape(whole)
    for i in range(hit_count):
        mixed = mixed + head_rows(shares[i] * scale, REQUESTS) * comb[i].reshape(whole).astype(jnp.float32)
    out[...] = mixed.astype(jnp.bfloat16).reshape(PER_DEV, HEADS, HD)

    def drained(d):
        query_copy(d, me).wait_send()
        out_copy(d, me).wait_send()
        lse_copy(d, me).wait_send()

    pl.loop(0, planes)(lambda j: peers(j, drained))
    for t in range(stages):
        kv_copy(t).wait_send()


def toggle(a, mask):
    out, bit = a, 1
    while bit <= mask:
        if mask & bit:
            out = out + bit - 2 * bit * ((a // bit) % 2)
        bit *= 2
    return out


def relay_kernel(n, prefix, hits, span, queries, fk, fv, ck, cv, out,
                 qin, qx, near_s, far_s, pack_s, near_in, far_in, pack_in, fwd, rel_in,
                 near_o, far_o, rel_o, relr, packr, back, near_l, far_l, rel_l, relr_l, packr_l, lback,
                 kv, kc, vc, pout, plse, comb, lcomb, firsts, lasts, doubled, chosen, owners, places,
                 nqs, nqr, fqs, fqr, wqs, wqr, nrs, nrr, frs, frr, wrs, wrr,
                 nls, nlr, fls, flr, wls, wlr, pqs, pqr, prs, prr, pls, plr, s1s, s1r, loc):
    me = lax.axis_index("cache")
    half = n // 2
    doubles = n // 4
    low = me % half
    side = me // half
    other = toggle(me, half)
    stages = int(math.log2(n))
    spot_me = mirrored(me, n)
    my_plane = (low // PLANE) * PLANE
    near_far = 2 * half
    packed = 3 * half

    loads = [
        pltpu.make_async_copy(queries, qin, loc.at[4]),
        pltpu.make_async_copy(fk, kv.at[spot_me, 0], loc.at[0]),
        pltpu.make_async_copy(fv, kv.at[spot_me, 1], loc.at[1]),
        pltpu.make_async_copy(ck, kc, loc.at[2]),
        pltpu.make_async_copy(cv, vc, loc.at[3]),
    ]
    for load in loads:
        load.start()

    barrier = pltpu.get_barrier_semaphore()
    for mask in reversed(range(1, n)):
        pl.semaphore_signal(barrier, inc=1, device_id={"cache": toggle(me, mask)}, device_id_type=MESH)

    for part in range(2):
        seen = jnp.int32(0)
        picks = [jnp.int32(0)] * doubles
        lows = [jnp.int32(0)] * doubles
        for spot in range(half):
            d = part * half + spot
            first = jnp.int32(REQUESTS - 1)
            last = jnp.int32(0)
            for r in reversed(range(REQUESTS)):
                first = jnp.where(hits[r] == d, r, first)
            for r in range(REQUESTS):
                last = jnp.where(hits[r] == d, r, last)
            firsts[d] = first
            lasts[d] = last
            doubled[d] = jnp.minimum(seen, doubles - 1)
            two = first < last
            for j in range(doubles):
                here = two & (seen == j)
                picks[j] = jnp.where(here, last, picks[j])
                lows[j] = jnp.where(here, spot, lows[j])
            seen = jnp.where(two, seen + 1, seen)
        for j in range(doubles):
            chosen[part * doubles + j] = picks[j]
            owners[part * doubles + j] = lows[j]

    for r in range(REQUESTS):
        owner = hits[r]
        second = firsts[owner] < r
        at_low = owner % half
        inside = 2 * at_low + jnp.where(second, 1, 0)
        outside = jnp.where(second, packed + doubled[owner], near_far + at_low)
        places[r] = jnp.where(owner // half == side, inside, outside)

    loads[0].wait()
    qx[...] = qin[...].reshape(REQUESTS, TOK, HEADS, HD)
    for j in range(doubles):
        pack_s[j] = qx[chosen[(1 - side) * doubles + j]]

    @pl.loop(0, half)
    def _(d):
        near_s[d, 0] = qx[firsts[side * half + d]]
        near_s[d, 1] = qx[lasts[side * half + d]]
        far_s[d] = qx[firsts[(1 - side) * half + d]]

    near_in[low] = near_s[low]
    for load in loads[1:]:
        load.wait()
    pl.semaphore_wait(barrier, n - 1)

    def remote(src, dst, sent, got, to):
        return pltpu.make_async_remote_copy(
            src_ref=src, dst_ref=dst, send_sem=sent, recv_sem=got,
            device_id={"cache": to}, device_id_type=MESH)

    def kv_copy(t, mine=True):
        size = 2**t
        start = (spot_me // size) * size
        if not mine:
            start = flip(spot_me // size, 1, n // size) * size
        block = kv.at[pl.ds(start, size)]
        return remote(block, block, s1s.at[t], s1r.at[t], toggle(me, n // (2 * size)))

    def inner(d):
        return side * half + d

    def outer(d):
        return (1 - side) * half + d

    def near_query(to, frm):
        return remote(near_s.at[to], near_in.at[frm], nqs.at[to], nqr.at[frm], inner(to))

    def far_query(to, frm):
        return remote(far_s.at[to], far_in.at[frm], fqs.at[to], fqr.at[frm], outer(to))

    def relay_query(to, frm):
        return remote(fwd.at[to], rel_in.at[frm], wqs.at[to], wqr.at[frm], inner(to))

    def near_out(to, frm):
        return (remote(near_o.at[to], back.at[pl.ds(2 * frm, 2)], nrs.at[to], nrr.at[frm], inner(to)),
                remote(near_l.at[to], lback.at[pl.ds(2 * frm, 2)], nls.at[to], nlr.at[frm], inner(to)))

    def far_out(to, frm):
        return (remote(far_o.at[to], back.at[near_far + frm], frs.at[to], frr.at[frm], outer(to)),
                remote(far_l.at[to], lback.at[near_far + frm], fls.at[to], flr.at[frm], outer(to)))

    def relay_out(to, frm):
        return (remote(rel_o.at[to], relr.at[frm], wrs.at[to], wrr.at[frm], inner(to)),
                remote(rel_l.at[to], relr_l.at[frm], wls.at[to], wlr.at[frm], inner(to)))

    pack_query = remote(pack_s, pack_in, pqs.at[0], pqr.at[0], other)
    pack_out = (remote(packr, back.at[pl.ds(packed, doubles)], prs.at[0], prr.at[0], other),
                remote(packr_l, lback.at[pl.ds(packed, doubles)], pls.at[0], plr.at[0], other))

    near_masks = list(range(1, half))
    plane_masks = list(range(1, PLANE))
    cross_masks = list(range(PLANE, half))

    limits = [prefix[firsts[me]], prefix[lasts[me]]]
    spot = lax.broadcasted_iota(jnp.int32, (1, REGION), 1)

    def answer(q, slot):
        part = pl.ds(slot * REGION, REGION)
        m, o = attend(q.reshape(ROWS, HD), kc[part], vc[part], spot < limits[slot])
        total = jnp.maximum(o[:, HD:], 1.0)
        lse = m * EXP2_SCALE + jnp.log2(total)
        result = (o[:, :HD] / total).astype(jnp.bfloat16)
        return result.reshape(PLANE, TOK, HEADS, HD), head_lanes(lse, PLANE, 0)

    def near_group(base, masks):
        for mask in masks:
            d = toggle(low, mask)
            near_query(d, d).wait_recv()
        group = pl.ds(base, PLANE)
        for slot in range(CAP):
            result, lanes = answer(near_in[group, slot], slot)
            near_o[group, slot] = result
            for k in range(PLANE):
                near_l[base + k, slot] = lanes[k:k + 1]

    def near_reply(masks):
        for mask in masks:
            for copy in near_out(toggle(low, mask), low):
                copy.start()

    def far_group(base, masks):
        for mask in masks:
            d = toggle(low, mask)
            far_query(d, d).wait_recv()
        group = pl.ds(base, PLANE)
        result, lanes = answer(far_in[group], 0)
        far_o[group] = result
        for k in range(PLANE):
            far_l[base + k] = lanes[k:k + 1]

    def far_reply(masks):
        for mask in masks:
            for copy in far_out(toggle(low, mask), low):
                copy.start()

    def relay_group(base, masks):
        for mask in masks:
            d = toggle(low, mask)
            relay_query(d, d).wait_recv()
        group = pl.ds(base, PLANE)
        result, lanes = answer(rel_in[group], 1)
        rel_o[group] = result
        for k in range(PLANE):
            rel_l[base + k] = lanes[k:k + 1]

    def relay_reply(masks):
        for mask in masks:
            for copy in relay_out(toggle(low, mask), low):
                copy.start()

    def next_kv(t):
        kv_copy(t, mine=False).wait_recv()
        kv_copy(t + 1).start()

    plane_next = toggle(low, PLANE) // PLANE * PLANE

    def far_start(masks):
        for mask in masks:
            far_query(toggle(low, mask), low).start()

    def near_start(masks):
        for mask in masks:
            near_query(toggle(low, mask), low).start()

    def forward():
        pack_query.wait_recv()

        @pl.loop(0, half)
        def _(d):
            fwd[d] = pack_in[doubled[side * half + d]]

        rel_in[low] = fwd[low]

    def forward_start(masks):
        for mask in masks:
            relay_query(toggle(low, mask), low).start()

    def gather_results():
        for mask in near_masks:
            d = toggle(low, mask)
            for copy in relay_out(d, d):
                copy.wait_recv()
        for j in range(doubles):
            packr[j] = relr[owners[side * doubles + j]]
            packr_l[j] = relr_l[owners[side * doubles + j]]

    def pack_reply():
        for copy in pack_out:
            copy.start()

    def prompt():
        span_f = span[...].astype(jnp.float32)
        mine = jnp.sum(
            jnp.where(lax.broadcasted_iota(jnp.int32, span_f.shape, 1) == me, span_f, 0.0),
            axis=1, keepdims=True)
        order = jnp.clip(span_f - mine, -1.0, 1.0).astype(jnp.bfloat16)
        reqs = ROWS // (TOK * HEADS)
        rows = reqs * TOK
        keys = n * rows
        key_lane = lax.broadcasted_iota(jnp.int32, (REQUESTS, keys), 1)
        key_row = lax.broadcasted_iota(jnp.int32, (REQUESTS, keys), 0)
        lane = lax.broadcasted_iota(jnp.int32, (n, keys), 1)
        dev = lax.broadcasted_iota(jnp.int32, (n, keys), 0)
        pick = jnp.where(mirrored(lane // rows, n) == dev, 1.0, 0.0).astype(jnp.bfloat16)
        step = jnp.dot(order, pick, preferred_element_type=jnp.float32)
        rank_all = step * TOK + (key_lane % TOK).astype(jnp.float32)
        token = ((lax.broadcasted_iota(jnp.int32, (ROWS, 1), 0) // HEADS) % TOK).astype(jnp.float32)
        row_at = lax.broadcasted_iota(jnp.int32, (ROWS, REQUESTS), 0) // (TOK * HEADS)
        req_at = lax.broadcasted_iota(jnp.int32, (ROWS, REQUESTS), 1)

        @pl.loop(0, REQUESTS // reqs)
        def _(c):
            same = (key_lane // TOK) % reqs + c * reqs == key_row
            rank = jnp.where(same, rank_all, 100.0).astype(jnp.bfloat16)
            spread = jnp.where(row_at + c * reqs == req_at, 1.0, 0.0).astype(jnp.bfloat16)
            ranked = jnp.dot(spread, rank, preferred_element_type=jnp.float32)
            part = pl.ds(pl.multiple_of(c * rows, rows), rows)
            m, o = attend(qx[pl.ds(c * reqs, reqs)].reshape(ROWS, HD), kv[:, 0, part].reshape(keys, HD),
                          kv[:, 1, part].reshape(keys, HD), ranked <= token)
            total = o[:, HD:]
            pout[pl.ds(pl.multiple_of(c * ROWS, ROWS), ROWS)] = o[:, :HD] / total
            plse[pl.ds(pl.multiple_of(c * reqs, reqs), reqs)] = head_lanes(m * EXP2_SCALE + jnp.log2(total), reqs, 0)


    near_start(plane_masks)
    near_start([PLANE + 0])
    near_start([PLANE + 1])
    near_start([PLANE + 2])
    kv_copy(0).start()
    near_start([PLANE + 3])
    pack_query.start()
    far_start([0])
    far_start([1])
    far_start([2])
    far_start([3])
    near_group(my_plane, plane_masks)
    back[pl.ds(2 * low, 2)] = near_o[low]
    lback[pl.ds(2 * low, 2)] = near_l[low]
    near_reply(plane_masks)
    next_kv(0)
    forward()
    forward_start(cross_masks)
    forward_start(plane_masks)
    far_start([PLANE + 3])
    far_start([PLANE + 2])
    far_start([PLANE + 1])
    far_start([PLANE + 0])
    near_group(plane_next, cross_masks)
    next_kv(1)
    near_reply(cross_masks)
    far_group(my_plane, [0] + plane_masks)
    far_reply([0] + plane_masks)
    relay_group(plane_next, cross_masks)
    relay_reply(cross_masks)
    relay_group(my_plane, plane_masks)
    relr[low] = rel_o[low]
    relr_l[low] = rel_l[low]
    relay_reply(plane_masks)
    far_group(plane_next, cross_masks)
    far_reply(cross_masks)
    next_kv(2)
    gather_results()
    pack_reply()
    kv_copy(stages - 1, mine=False).wait_recv()
    prompt()

    for mask in near_masks:
        d = toggle(low, mask)
        for copy in near_out(d, d):
            copy.wait_recv()
    for mask in range(half):
        d = toggle(low, mask)
        for copy in far_out(d, d):
            copy.wait_recv()
    for copy in pack_out:
        copy.wait_recv()

    for r in range(REQUESTS):
        comb[r] = back[places[r]]
        lcomb[r:r + 1] = lback[places[r]]
    top = jnp.maximum(plse[...], lcomb[...])
    share = jnp.exp2(plse[...] - top)
    taken = jnp.exp2(lcomb[...] - top)
    weight = head_rows(taken / (share + taken), REQUESTS)
    whole = (REQUESTS, TOK * HEADS, HD)
    fresh = pout[...].reshape(whole)
    mixed = fresh + weight * (comb[...].reshape(whole).astype(jnp.float32) - fresh)
    pout[...] = mixed.reshape(PER_DEV * HEADS, HD)
    for h in range(HEADS):
        out[:, h * HD:(h + 1) * HD] = pout[pl.ds(h, PER_DEV, stride=HEADS)].astype(jnp.bfloat16)

    pack_query.wait_send()
    for mask in [0] + plane_masks:
        far_query(toggle(low, mask), low).wait_send()
    for mask in cross_masks:
        near_query(toggle(low, mask), low).wait_send()
    for mask in cross_masks:
        far_query(toggle(low, mask), low).wait_send()
    for mask in plane_masks:
        near_query(toggle(low, mask), low).wait_send()
    for mask in range(half):
        for copy in far_out(toggle(low, mask), low):
            copy.wait_send()
    for mask in near_masks:
        d = toggle(low, mask)
        relay_query(d, low).wait_send()
        for copy in near_out(d, low) + relay_out(d, low):
            copy.wait_send()
    for copy in pack_out:
        copy.wait_send()
    for t in range(0, stages):
        kv_copy(t).wait_send()


def relay_scratch(n):
    bf16, f32 = jnp.bfloat16, jnp.float32
    dma = pltpu.SemaphoreType.DMA
    half, doubles = n // 2, n // 4
    block = (TOK, HEADS, HD)

    def blocks(*lead):
        return pltpu.VMEM(lead + block, bf16)

    def lanes(*lead):
        return pltpu.VMEM(lead + (1, HD), f32)

    results = 3 * half + doubles
    return [
        pltpu.VMEM((PER_DEV, HEADS * HD), bf16), blocks(REQUESTS),
        blocks(half, CAP), blocks(half), blocks(doubles), blocks(half, CAP), blocks(half), blocks(doubles), blocks(half), blocks(half),
        blocks(half, CAP), blocks(half), blocks(half), blocks(half), blocks(doubles), blocks(results),
        lanes(half, CAP), lanes(half), lanes(half), lanes(half), lanes(doubles), lanes(results),
        pltpu.VMEM((n, 2, PER_DEV, HD), bf16),
        pltpu.VMEM((CAP * REGION, HD), bf16), pltpu.VMEM((CAP * REGION, HD), bf16),
        pltpu.VMEM((PER_DEV * HEADS, HD), f32), pltpu.VMEM((REQUESTS, HD), f32),
        blocks(REQUESTS), pltpu.VMEM((REQUESTS, HD), f32),
    ] + [pltpu.SMEM((size,), jnp.int32) for size in (n, n, n, 2 * doubles, 2 * doubles, REQUESTS)
    ] + [dma((half,))] * 18 + [dma((1,))] * 6 + [dma((int(math.log2(n)),))] * 2 + [dma((5,))]


def direct_scratch(n, hit_count):
    bf16, f32 = jnp.bfloat16, jnp.float32
    dma = pltpu.SemaphoreType.DMA
    block = (n, CAP, TOK, HEADS, HD)
    return [
        pltpu.VMEM((PER_DEV, HEADS * HD), bf16), pltpu.VMEM((REQUESTS, TOK, HEADS, HD), bf16),
        pltpu.VMEM(block, bf16), pltpu.VMEM(block, bf16),
        pltpu.VMEM(block, bf16), pltpu.VMEM(block, bf16),
        pltpu.VMEM((n, 1, HD), f32), pltpu.VMEM((n, 1, HD), f32),
        pltpu.VMEM((n, 2, PER_DEV, HD), bf16),
        pltpu.VMEM((CAP * REGION, HD), bf16), pltpu.VMEM((CAP * REGION, HD), bf16),
        pltpu.VMEM((REQUESTS, TOK, HEADS, HD), f32), pltpu.VMEM((REQUESTS, HD), f32),
        pltpu.VMEM((hit_count, REQUESTS, TOK, HEADS, HD), bf16),
        pltpu.VMEM((hit_count, REQUESTS, HD), f32),
    ] + [dma((n,))] * 6 + [dma((int(math.log2(n)),))] * 2 + [dma((5,))]


def solution(mesh):
    n = mesh.shape["cache"]

    def body(prefix_len, hits, span_block, queries, fresh_keys, fresh_values, cache_keys, cache_values):
        hit_count = hits.shape[1]
        vmem = pl.BlockSpec(memory_space=pltpu.VMEM)
        smem = pl.BlockSpec(memory_space=pltpu.SMEM)
        hbm = pl.BlockSpec(memory_space=pltpu.HBM)
        if hit_count == 1 and n // 2 == CAP * PLANE:
            program, scratch, shape = functools.partial(relay_kernel, n), relay_scratch(n), (PER_DEV, HEADS * HD)
        else:
            program, scratch = functools.partial(kernel, n, hit_count), direct_scratch(n, hit_count)
            shape = (PER_DEV, HEADS, HD)
        result = pl.pallas_call(
            program,
            out_shape=pltpu.VMEM(shape, jnp.bfloat16),
            in_specs=[smem, smem, vmem, hbm, hbm, hbm, hbm, hbm],
            out_specs=vmem,
            scratch_shapes=scratch,
            compiler_params=pltpu.CompilerParams(
                collective_id=0, has_side_effects=True, vmem_limit_bytes=60 << 20),
        )(prefix_len, hits.reshape(-1), span_block, queries, fresh_keys, fresh_values, cache_keys, cache_values)
        return result.reshape(PER_DEV, HEADS * HD)

    in_specs = (
        P("groups"), P("groups", None), P("groups", None),
        P(("groups", "cache"), None), P(("groups", "cache"), None), P(("groups", "cache"), None),
        P(("groups", "cache"), None), P(("groups", "cache"), None),
    )
    return jax.shard_map(body, mesh=mesh, in_specs=in_specs,
                         out_specs=P(("groups", "cache"), None), check_vma=False)
```

```python
import functools
import math

import jax
import jax.numpy as jnp
from jax import lax
from jax.experimental import pallas as pl
from jax.experimental.pallas import tpu as pltpu
from jax.sharding import PartitionSpec as P

HEADS = 16
HD = 128
PAGE = 128
CAP = 2
REQUESTS = 16
TOK = 4
PAGES_DEV = 16
REGION = PAGES_DEV // CAP * PAGE
PER_DEV = REQUESTS * TOK
PLANE = 4
ROWS = PLANE * TOK * HEADS
MESH = pl.DeviceIdType.MESH
FLOOR = -1e30
EXP2_SCALE = HD**-0.5 * math.log2(math.e)


def flip(a, b, size):
    out, bit = 0, 1
    while bit < size:
        out = out + ((a // bit + b // bit) % 2) * bit
        bit *= 2
    return out


def attend(q, k, v, visible):
    s = lax.dot_general(q, k, (((1,), (1,)), ((), ())), preferred_element_type=jnp.float32)
    s = jnp.where(visible, s, FLOOR)
    m = jnp.max(s, axis=1, keepdims=True)
    p = jnp.exp2((s - m) * EXP2_SCALE).astype(jnp.bfloat16)
    v1 = jnp.concatenate([v, jnp.ones_like(v)], axis=1)
    o = jnp.dot(p, v1, preferred_element_type=jnp.float32)
    return m, o


def head_lanes(x, units, first):
    row = lax.broadcasted_iota(jnp.int32, (units, TOK * HEADS, HD), 1)
    lane = lax.broadcasted_iota(jnp.int32, (units, TOK * HEADS, HD), 2)
    wide = x.reshape(units, TOK * HEADS, HD)
    return jnp.sum(jnp.where(row + first == lane, wide, 0.0), axis=1)


def head_rows(x, units):
    row = lax.broadcasted_iota(jnp.int32, (units, TOK * HEADS, HD), 1)
    lane = lax.broadcasted_iota(jnp.int32, (units, TOK * HEADS, HD), 2)
    wide = jnp.broadcast_to(x[:, None, :], (units, TOK * HEADS, HD))
    return jnp.sum(jnp.where(row == lane, wide, 0.0), axis=2, keepdims=True)


def mirrored(a, size):
    out, bit = 0, 1
    while bit < size:
        out = out + ((a // bit) % 2) * (size // (2 * bit))
        bit *= 2
    return out


def kernel(n, hit_count, prefix, hits, span, queries, fk, fv, ck, cv, out,
           qin, qx, send, arrived, ret, back, lret, lback, kv, kc, vc, pout, plse, comb, lcomb,
           qs, qr, rs, rr, ls, lr, s1s, s1r, loc):
    me = lax.axis_index("cache")
    planes = n // PLANE
    stages = int(math.log2(n))
    spot_me = mirrored(me, n)
    my_plane = me // PLANE

    loads = [
        pltpu.make_async_copy(queries, qin, loc.at[4]),
        pltpu.make_async_copy(fk, kv.at[spot_me, 0], loc.at[0]),
        pltpu.make_async_copy(fv, kv.at[spot_me, 1], loc.at[1]),
        pltpu.make_async_copy(ck, kc, loc.at[2]),
        pltpu.make_async_copy(cv, vc, loc.at[3]),
    ]
    for load in loads:
        load.start()

    barrier = pltpu.get_barrier_semaphore()

    @pl.loop(1, n)
    def _(k):
        pl.semaphore_signal(barrier, inc=1, device_id={"cache": (me + k) % n}, device_id_type=MESH)

    def named_by(d):
        first = jnp.int32(REQUESTS - 1)
        last = jnp.int32(0)
        for r in range(REQUESTS):
            for i in range(hit_count):
                here = hits[r * hit_count + i] == d
                first = jnp.where(here, jnp.minimum(first, r), first)
                last = jnp.where(here, r, last)
        return first, last

    loads[0].wait()
    qx[...] = qin[...].reshape(REQUESTS, TOK, HEADS, HD)

    @pl.loop(0, n)
    def _(d):
        first, last = named_by(d)
        send[d, 0] = qx[first]
        send[d, 1] = qx[last]

    pl.semaphore_wait(barrier, n - 1)
    loads[1].wait()
    loads[2].wait()

    def kv_copy(t, mine=True):
        size = 2**t
        start = (spot_me // size) * size
        if not mine:
            start = flip(spot_me // size, 1, n // size) * size
        block = kv.at[pl.ds(start, size)]
        return pltpu.make_async_remote_copy(
            src_ref=block, dst_ref=block, send_sem=s1s.at[t], recv_sem=s1r.at[t],
            device_id={"cache": flip(me, n // (2 * size), n)}, device_id_type=MESH)

    kv_copy(0).start()

    def query_copy(to, frm):
        return pltpu.make_async_remote_copy(
            src_ref=send.at[to], dst_ref=arrived.at[frm], send_sem=qs.at[to], recv_sem=qr.at[frm],
            device_id={"cache": to}, device_id_type=MESH)

    def out_copy(to, frm):
        return pltpu.make_async_remote_copy(
            src_ref=ret.at[to], dst_ref=back.at[frm], send_sem=rs.at[to], recv_sem=rr.at[frm],
            device_id={"cache": to}, device_id_type=MESH)

    def lse_copy(to, frm):
        return pltpu.make_async_remote_copy(
            src_ref=lret.at[to], dst_ref=lback.at[frm], send_sem=ls.at[to], recv_sem=lr.at[frm],
            device_id={"cache": to}, device_id_type=MESH)

    def peers(j, act):
        base = flip(my_plane, j, planes) * PLANE

        @pl.loop(0, PLANE)
        def _(k):
            d = base + (me + k) % PLANE

            @pl.when(d != me)
            def _():
                act(d)

    @pl.loop(0, planes)
    def _(i):
        peers((i + 1) % planes, lambda d: query_copy(d, me).start())

    arrived[me] = send[me]
    loads[3].wait()
    loads[4].wait()

    limits = []
    for request in named_by(me):
        place = jnp.int32(0)
        for i in range(hit_count):
            place = jnp.where(hits[request * hit_count + i] == me, i, place)
        limits.append(prefix[request] - place * REGION)
    spot = lax.broadcasted_iota(jnp.int32, (1, REGION), 1)

    def serve(j):
        peers(j, lambda d: query_copy(d, d).wait_recv())
        base = flip(my_plane, j, planes) * PLANE
        lanes = jnp.zeros((PLANE, HD), jnp.float32)

        for slot in range(CAP):
            q = arrived[pl.ds(base, PLANE), slot].reshape(ROWS, HD)
            part = pl.ds(slot * REGION, REGION)
            m, o = attend(q, kc[part], vc[part], spot < limits[slot])
            total = jnp.maximum(o[:, HD:], 1.0)
            lse = m * EXP2_SCALE + jnp.log2(total)
            lse = jnp.where(limits[slot] > 0, lse, FLOOR)
            result = (o[:, :HD] / total).astype(jnp.bfloat16)
            ret[pl.ds(base, PLANE), slot] = result.reshape(PLANE, TOK, HEADS, HD)
            lanes = lanes + head_lanes(lse, PLANE, slot * TOK * HEADS)
        for k in range(PLANE):
            lret[base + k] = lanes[k:k + 1]

        def go(d):
            out_copy(d, me).start()
            lse_copy(d, me).start()

        peers(j, go)

        for t in range(stages - 1):
            @pl.when(j == t)
            def _():
                kv_copy(t, mine=False).wait_recv()
                kv_copy(t + 1).start()

    pl.loop(0, planes)(serve)
    back[me] = ret[me]
    lback[me] = lret[me]
    kv_copy(stages - 1, mine=False).wait_recv()

    span_f = span[...].astype(jnp.float32)
    mine = jnp.sum(
        jnp.where(lax.broadcasted_iota(jnp.int32, span_f.shape, 1) == me, span_f, 0.0),
        axis=1, keepdims=True)
    order = jnp.clip(span_f - mine, -1.0, 1.0).astype(jnp.bfloat16)
    group = 16
    keys = group * PER_DEV
    chunks = n // group
    key_lane = lax.broadcasted_iota(jnp.int32, (REQUESTS, keys), 1)
    key_row = lax.broadcasted_iota(jnp.int32, (REQUESTS, keys), 0)

    def ranks(chunk):
        lane = lax.broadcasted_iota(jnp.int32, (n, keys), 1)
        dev = lax.broadcasted_iota(jnp.int32, (n, keys), 0)
        pick = jnp.where(mirrored(lane // PER_DEV + chunk * group, n) == dev, 1.0, 0.0).astype(jnp.bfloat16)
        step = jnp.dot(order, pick, preferred_element_type=jnp.float32)
        spot_rank = step * TOK + (key_lane % TOK).astype(jnp.float32)
        same = (key_lane // TOK) % REQUESTS == key_row
        return jnp.where(same, spot_rank, 100.0).astype(jnp.bfloat16)

    def kv_rows(chunk, which):
        return kv[pl.ds(chunk * group, group), which].reshape(keys, HD)

    def prompt_part(c, chunk, rank):
        q = qx_rows(c)
        row = lax.broadcasted_iota(jnp.int32, (ROWS, REQUESTS), 0)
        req = lax.broadcasted_iota(jnp.int32, (ROWS, REQUESTS), 1)
        spread = jnp.where(row // (TOK * HEADS) + c * (ROWS // (TOK * HEADS)) == req, 1.0, 0.0)
        ranked = jnp.dot(spread.astype(jnp.bfloat16), rank, preferred_element_type=jnp.float32)
        token = (lax.broadcasted_iota(jnp.int32, (ROWS, 1), 0) // HEADS) % TOK
        return attend(q, kv_rows(chunk, 0), kv_rows(chunk, 1), ranked <= token.astype(jnp.float32))

    reqs = ROWS // (TOK * HEADS)

    def qx_rows(c):
        return qx[pl.ds(c * reqs, reqs)].reshape(ROWS, HD)

    rank0 = ranks(0) if chunks == 1 else None

    @pl.loop(0, REQUESTS // reqs)
    def _(c):
        if chunks == 1:
            m, o = prompt_part(c, 0, rank0)
        else:
            def more(chunk, carry):
                m0, o0 = carry
                m1, o1 = prompt_part(c, chunk, ranks(chunk))
                m2 = jnp.maximum(m0, m1)
                return m2, (o0 * jnp.exp2((m0 - m2) * EXP2_SCALE)
                            + o1 * jnp.exp2((m1 - m2) * EXP2_SCALE))
            m, o = lax.fori_loop(0, chunks, more, (
                jnp.full((ROWS, 1), FLOOR, jnp.float32), jnp.zeros((ROWS, 2 * HD), jnp.float32)))
        total = o[:, HD:]
        pout[pl.ds(c * reqs, reqs)] = (o[:, :HD] / total).reshape(reqs, TOK, HEADS, HD)
        plse[pl.ds(pl.multiple_of(c * reqs, reqs), reqs)] = head_lanes(m * EXP2_SCALE + jnp.log2(total), reqs, 0)

    def finish(d):
        out_copy(d, d).wait_recv()
        lse_copy(d, d).wait_recv()

    pl.loop(0, planes)(lambda j: peers(j, finish))

    for i in range(hit_count):
        for r in range(REQUESTS):
            owner = hits[r * hit_count + i]
            rank = jnp.int32(0)
            for r2 in range(r):
                for i2 in range(hit_count):
                    rank = jnp.where(hits[r2 * hit_count + i2] == owner, rank + 1, rank)
            rank = jnp.minimum(rank, CAP - 1)
            comb[i, r] = back[owner, rank]
            row = lback[owner]
            lcomb[i, r:r + 1] = jnp.where(rank == 0, row, pltpu.roll(row, HD // 2, 1))

    top = plse[...]
    for i in range(hit_count):
        top = jnp.maximum(top, lcomb[i])
    share = jnp.exp2(plse[...] - top)
    shares = [jnp.exp2(lcomb[i] - top) for i in range(hit_count)]
    scale = 1.0 / functools.reduce(jnp.add, shares, share)
    whole = (REQUESTS, TOK * HEADS, HD)
    mixed = head_rows(share * scale, REQUESTS) * pout[...].reshape(whole)
    for i in range(hit_count):
        mixed = mixed + head_rows(shares[i] * scale, REQUESTS) * comb[i].reshape(whole).astype(jnp.float32)
    out[...] = mixed.astype(jnp.bfloat16).reshape(PER_DEV, HEADS, HD)

    def drained(d):
        query_copy(d, me).wait_send()
        out_copy(d, me).wait_send()
        lse_copy(d, me).wait_send()

    pl.loop(0, planes)(lambda j: peers(j, drained))
    for t in range(stages):
        kv_copy(t).wait_send()


def toggle(a, mask):
    out, bit = a, 1
    while bit <= mask:
        if mask & bit:
            out = out + bit - 2 * bit * ((a // bit) % 2)
        bit *= 2
    return out


def relay_kernel(n, prefix, hits, span, queries, fk, fv, ck, cv, out,
                 qin, qx, near_s, far_s, pack_s, near_in, far_in, pack_in, fwd, rel_in,
                 near_o, far_o, rel_o, relr, packr, back, near_l, far_l, rel_l, relr_l, packr_l, lback,
                 kv, kc, vc, pout, plse, comb, lcomb, firsts, lasts, doubled, chosen, owners, places,
                 nqs, nqr, fqs, fqr, wqs, wqr, nrs, nrr, frs, frr, wrs, wrr,
                 nls, nlr, fls, flr, wls, wlr, pqs, pqr, prs, prr, pls, plr, s1s, s1r, loc):
    me = lax.axis_index("cache")
    half = n // 2
    doubles = n // 4
    low = me % half
    side = me // half
    other = toggle(me, half)
    stages = int(math.log2(n))
    spot_me = mirrored(me, n)
    my_plane = (low // PLANE) * PLANE
    near_far = 2 * half
    packed = 3 * half

    loads = [
        pltpu.make_async_copy(queries, qin, loc.at[4]),
        pltpu.make_async_copy(fk, kv.at[spot_me, 0], loc.at[0]),
        pltpu.make_async_copy(fv, kv.at[spot_me, 1], loc.at[1]),
        pltpu.make_async_copy(ck, kc, loc.at[2]),
        pltpu.make_async_copy(cv, vc, loc.at[3]),
    ]
    for load in loads:
        load.start()

    barrier = pltpu.get_barrier_semaphore()
    for mask in reversed(range(1, n)):
        pl.semaphore_signal(barrier, inc=1, device_id={"cache": toggle(me, mask)}, device_id_type=MESH)

    for part in range(2):
        seen = jnp.int32(0)
        picks = [jnp.int32(0)] * doubles
        lows = [jnp.int32(0)] * doubles
        for spot in range(half):
            d = part * half + spot
            first = jnp.int32(REQUESTS - 1)
            last = jnp.int32(0)
            for r in reversed(range(REQUESTS)):
                first = jnp.where(hits[r] == d, r, first)
            for r in range(REQUESTS):
                last = jnp.where(hits[r] == d, r, last)
            firsts[d] = first
            lasts[d] = last
            doubled[d] = jnp.minimum(seen, doubles - 1)
            two = first < last
            for j in range(doubles):
                here = two & (seen == j)
                picks[j] = jnp.where(here, last, picks[j])
                lows[j] = jnp.where(here, spot, lows[j])
            seen = jnp.where(two, seen + 1, seen)
        for j in range(doubles):
            chosen[part * doubles + j] = picks[j]
            owners[part * doubles + j] = lows[j]

    for r in range(REQUESTS):
        owner = hits[r]
        second = firsts[owner] < r
        at_low = owner % half
        inside = 2 * at_low + jnp.where(second, 1, 0)
        outside = jnp.where(second, packed + doubled[owner], near_far + at_low)
        places[r] = jnp.where(owner // half == side, inside, outside)

    loads[0].wait()
    qx[...] = qin[...].reshape(REQUESTS, TOK, HEADS, HD)
    for j in range(doubles):
        pack_s[j] = qx[chosen[(1 - side) * doubles + j]]

    @pl.loop(0, half)
    def _(d):
        near_s[d, 0] = qx[firsts[side * half + d]]
        near_s[d, 1] = qx[lasts[side * half + d]]
        far_s[d] = qx[firsts[(1 - side) * half + d]]

    near_in[low] = near_s[low]
    for load in loads[1:]:
        load.wait()
    pl.semaphore_wait(barrier, n - 1)

    def remote(src, dst, sent, got, to):
        return pltpu.make_async_remote_copy(
            src_ref=src, dst_ref=dst, send_sem=sent, recv_sem=got,
            device_id={"cache": to}, device_id_type=MESH)

    def kv_copy(t, mine=True):
        size = 2**t
        start = (spot_me // size) * size
        if not mine:
            start = flip(spot_me // size, 1, n // size) * size
        block = kv.at[pl.ds(start, size)]
        return remote(block, block, s1s.at[t], s1r.at[t], toggle(me, n // (2 * size)))

    def inner(d):
        return side * half + d

    def outer(d):
        return (1 - side) * half + d

    def near_query(to, frm):
        return remote(near_s.at[to], near_in.at[frm], nqs.at[to], nqr.at[frm], inner(to))

    def far_query(to, frm):
        return remote(far_s.at[to], far_in.at[frm], fqs.at[to], fqr.at[frm], outer(to))

    def relay_query(to, frm):
        return remote(fwd.at[to], rel_in.at[frm], wqs.at[to], wqr.at[frm], inner(to))

    def near_out(to, frm):
        return (remote(near_o.at[to], back.at[pl.ds(2 * frm, 2)], nrs.at[to], nrr.at[frm], inner(to)),
                remote(near_l.at[to], lback.at[pl.ds(2 * frm, 2)], nls.at[to], nlr.at[frm], inner(to)))

    def far_out(to, frm):
        return (remote(far_o.at[to], back.at[near_far + frm], frs.at[to], frr.at[frm], outer(to)),
                remote(far_l.at[to], lback.at[near_far + frm], fls.at[to], flr.at[frm], outer(to)))

    def relay_out(to, frm):
        return (remote(rel_o.at[to], relr.at[frm], wrs.at[to], wrr.at[frm], inner(to)),
                remote(rel_l.at[to], relr_l.at[frm], wls.at[to], wlr.at[frm], inner(to)))

    pack_query = remote(pack_s, pack_in, pqs.at[0], pqr.at[0], other)
    pack_out = (remote(packr, back.at[pl.ds(packed, doubles)], prs.at[0], prr.at[0], other),
                remote(packr_l, lback.at[pl.ds(packed, doubles)], pls.at[0], plr.at[0], other))

    near_masks = list(range(1, half))
    plane_masks = list(range(1, PLANE))
    cross_masks = list(range(PLANE, half))

    limits = [prefix[firsts[me]], prefix[lasts[me]]]
    spot = lax.broadcasted_iota(jnp.int32, (1, REGION), 1)

    def answer(q, slot):
        part = pl.ds(slot * REGION, REGION)
        m, o = attend(q.reshape(ROWS, HD), kc[part], vc[part], spot < limits[slot])
        total = jnp.maximum(o[:, HD:], 1.0)
        lse = m * EXP2_SCALE + jnp.log2(total)
        result = (o[:, :HD] / total).astype(jnp.bfloat16)
        return result.reshape(PLANE, TOK, HEADS, HD), head_lanes(lse, PLANE, 0)

    def near_group(base, masks):
        for mask in masks:
            d = toggle(low, mask)
            near_query(d, d).wait_recv()
        group = pl.ds(base, PLANE)
        for slot in range(CAP):
            result, lanes = answer(near_in[group, slot], slot)
            near_o[group, slot] = result
            for k in range(PLANE):
                near_l[base + k, slot] = lanes[k:k + 1]

    def near_reply(masks):
        for mask in masks:
            for copy in near_out(toggle(low, mask), low):
                copy.start()

    def far_group(base, masks):
        for mask in masks:
            d = toggle(low, mask)
            far_query(d, d).wait_recv()
        group = pl.ds(base, PLANE)
        result, lanes = answer(far_in[group], 0)
        far_o[group] = result
        for k in range(PLANE):
            far_l[base + k] = lanes[k:k + 1]

    def far_reply(masks):
        for mask in masks:
            for copy in far_out(toggle(low, mask), low):
                copy.start()

    def relay_group(base, masks):
        for mask in masks:
            d = toggle(low, mask)
            relay_query(d, d).wait_recv()
        group = pl.ds(base, PLANE)
        result, lanes = answer(rel_in[group], 1)
        rel_o[group] = result
        for k in range(PLANE):
            rel_l[base + k] = lanes[k:k + 1]

    def relay_reply(masks):
        for mask in masks:
            for copy in relay_out(toggle(low, mask), low):
                copy.start()

    def next_kv(t):
        kv_copy(t, mine=False).wait_recv()
        kv_copy(t + 1).start()

    plane_next = toggle(low, PLANE) // PLANE * PLANE

    def far_start(masks):
        for mask in masks:
            far_query(toggle(low, mask), low).start()

    def near_start(masks):
        for mask in masks:
            near_query(toggle(low, mask), low).start()

    def forward():
        pack_query.wait_recv()

        @pl.loop(0, half)
        def _(d):
            fwd[d] = pack_in[doubled[side * half + d]]

        rel_in[low] = fwd[low]

    def forward_start(masks):
        for mask in masks:
            relay_query(toggle(low, mask), low).start()

    def gather_results():
        for mask in near_masks:
            d = toggle(low, mask)
            for copy in relay_out(d, d):
                copy.wait_recv()
        for j in range(doubles):
            packr[j] = relr[owners[side * doubles + j]]
            packr_l[j] = relr_l[owners[side * doubles + j]]

    def pack_reply():
        for copy in pack_out:
            copy.start()

    def prompt():
        span_f = span[...].astype(jnp.float32)
        mine = jnp.sum(
            jnp.where(lax.broadcasted_iota(jnp.int32, span_f.shape, 1) == me, span_f, 0.0),
            axis=1, keepdims=True)
        order = jnp.clip(span_f - mine, -1.0, 1.0).astype(jnp.bfloat16)
        reqs = ROWS // (TOK * HEADS)
        rows = reqs * TOK
        keys = n * rows
        key_lane = lax.broadcasted_iota(jnp.int32, (REQUESTS, keys), 1)
        key_row = lax.broadcasted_iota(jnp.int32, (REQUESTS, keys), 0)
        lane = lax.broadcasted_iota(jnp.int32, (n, keys), 1)
        dev = lax.broadcasted_iota(jnp.int32, (n, keys), 0)
        pick = jnp.where(mirrored(lane // rows, n) == dev, 1.0, 0.0).astype(jnp.bfloat16)
        step = jnp.dot(order, pick, preferred_element_type=jnp.float32)
        rank_all = step * TOK + (key_lane % TOK).astype(jnp.float32)
        token = ((lax.broadcasted_iota(jnp.int32, (ROWS, 1), 0) // HEADS) % TOK).astype(jnp.float32)
        row_at = lax.broadcasted_iota(jnp.int32, (ROWS, REQUESTS), 0) // (TOK * HEADS)
        req_at = lax.broadcasted_iota(jnp.int32, (ROWS, REQUESTS), 1)

        @pl.loop(0, REQUESTS // reqs)
        def _(c):
            same = (key_lane // TOK) % reqs + c * reqs == key_row
            rank = jnp.where(same, rank_all, 100.0).astype(jnp.bfloat16)
            spread = jnp.where(row_at + c * reqs == req_at, 1.0, 0.0).astype(jnp.bfloat16)
            ranked = jnp.dot(spread, rank, preferred_element_type=jnp.float32)
            part = pl.ds(pl.multiple_of(c * rows, rows), rows)
            m, o = attend(qx[pl.ds(c * reqs, reqs)].reshape(ROWS, HD), kv[:, 0, part].reshape(keys, HD),
                          kv[:, 1, part].reshape(keys, HD), ranked <= token)
            total = o[:, HD:]
            pout[pl.ds(pl.multiple_of(c * ROWS, ROWS), ROWS)] = o[:, :HD] / total
            plse[pl.ds(pl.multiple_of(c * reqs, reqs), reqs)] = head_lanes(m * EXP2_SCALE + jnp.log2(total), reqs, 0)


    near_start(plane_masks)
    near_start([PLANE + 0])
    near_start([PLANE + 1])
    near_start([PLANE + 2])
    kv_copy(0).start()
    near_start([PLANE + 3])
    pack_query.start()
    far_start([0])
    far_start([1])
    far_start([2])
    far_start([3])
    near_group(my_plane, plane_masks)
    back[pl.ds(2 * low, 2)] = near_o[low]
    lback[pl.ds(2 * low, 2)] = near_l[low]
    near_reply(plane_masks)
    next_kv(0)
    forward()
    forward_start(cross_masks)
    forward_start(plane_masks)
    far_start([PLANE + 3])
    far_start([PLANE + 2])
    far_start([PLANE + 1])
    far_start([PLANE + 0])
    near_group(plane_next, cross_masks)
    next_kv(1)
    near_reply(cross_masks)
    far_group(my_plane, [0] + plane_masks)
    far_reply([0] + plane_masks)
    relay_group(plane_next, cross_masks)
    relay_reply(cross_masks)
    relay_group(my_plane, plane_masks)
    relr[low] = rel_o[low]
    relr_l[low] = rel_l[low]
    relay_reply(plane_masks)
    far_group(plane_next, cross_masks)
    far_reply(cross_masks)
    next_kv(2)
    kv_copy(stages - 1, mine=False).wait_recv()
    gather_results()
    pack_reply()
    prompt()

    for mask in near_masks:
        d = toggle(low, mask)
        for copy in near_out(d, d):
            copy.wait_recv()
    for mask in range(half):
        d = toggle(low, mask)
        for copy in far_out(d, d):
            copy.wait_recv()
    for copy in pack_out:
        copy.wait_recv()

    for r in range(REQUESTS):
        comb[r] = back[places[r]]
        lcomb[r:r + 1] = lback[places[r]]
    top = jnp.maximum(plse[...], lcomb[...])
    share = jnp.exp2(plse[...] - top)
    taken = jnp.exp2(lcomb[...] - top)
    weight = head_rows(taken / (share + taken), REQUESTS)
    whole = (REQUESTS, TOK * HEADS, HD)
    fresh = pout[...].reshape(whole)
    mixed = fresh + weight * (comb[...].reshape(whole).astype(jnp.float32) - fresh)
    pout[...] = mixed.reshape(PER_DEV * HEADS, HD)
    for h in range(HEADS):
        out[:, h * HD:(h + 1) * HD] = pout[pl.ds(h, PER_DEV, stride=HEADS)].astype(jnp.bfloat16)

    pack_query.wait_send()
    for mask in [0] + plane_masks:
        far_query(toggle(low, mask), low).wait_send()
    for mask in cross_masks:
        near_query(toggle(low, mask), low).wait_send()
    for mask in cross_masks:
        far_query(toggle(low, mask), low).wait_send()
    for mask in plane_masks:
        near_query(toggle(low, mask), low).wait_send()
    for mask in range(half):
        for copy in far_out(toggle(low, mask), low):
            copy.wait_send()
    for mask in near_masks:
        d = toggle(low, mask)
        relay_query(d, low).wait_send()
        for copy in near_out(d, low) + relay_out(d, low):
            copy.wait_send()
    for copy in pack_out:
        copy.wait_send()
    for t in range(0, stages):
        kv_copy(t).wait_send()


def relay_scratch(n):
    bf16, f32 = jnp.bfloat16, jnp.float32
    dma = pltpu.SemaphoreType.DMA
    half, doubles = n // 2, n // 4
    block = (TOK, HEADS, HD)

    def blocks(*lead):
        return pltpu.VMEM(lead + block, bf16)

    def lanes(*lead):
        return pltpu.VMEM(lead + (1, HD), f32)

    results = 3 * half + doubles
    return [
        pltpu.VMEM((PER_DEV, HEADS * HD), bf16), blocks(REQUESTS),
        blocks(half, CAP), blocks(half), blocks(doubles), blocks(half, CAP), blocks(half), blocks(doubles), blocks(half), blocks(half),
        blocks(half, CAP), blocks(half), blocks(half), blocks(half), blocks(doubles), blocks(results),
        lanes(half, CAP), lanes(half), lanes(half), lanes(half), lanes(doubles), lanes(results),
        pltpu.VMEM((n, 2, PER_DEV, HD), bf16),
        pltpu.VMEM((CAP * REGION, HD), bf16), pltpu.VMEM((CAP * REGION, HD), bf16),
        pltpu.VMEM((PER_DEV * HEADS, HD), f32), pltpu.VMEM((REQUESTS, HD), f32),
        blocks(REQUESTS), pltpu.VMEM((REQUESTS, HD), f32),
    ] + [pltpu.SMEM((size,), jnp.int32) for size in (n, n, n, 2 * doubles, 2 * doubles, REQUESTS)
    ] + [dma((half,))] * 18 + [dma((1,))] * 6 + [dma((int(math.log2(n)),))] * 2 + [dma((5,))]


def direct_scratch(n, hit_count):
    bf16, f32 = jnp.bfloat16, jnp.float32
    dma = pltpu.SemaphoreType.DMA
    block = (n, CAP, TOK, HEADS, HD)
    return [
        pltpu.VMEM((PER_DEV, HEADS * HD), bf16), pltpu.VMEM((REQUESTS, TOK, HEADS, HD), bf16),
        pltpu.VMEM(block, bf16), pltpu.VMEM(block, bf16),
        pltpu.VMEM(block, bf16), pltpu.VMEM(block, bf16),
        pltpu.VMEM((n, 1, HD), f32), pltpu.VMEM((n, 1, HD), f32),
        pltpu.VMEM((n, 2, PER_DEV, HD), bf16),
        pltpu.VMEM((CAP * REGION, HD), bf16), pltpu.VMEM((CAP * REGION, HD), bf16),
        pltpu.VMEM((REQUESTS, TOK, HEADS, HD), f32), pltpu.VMEM((REQUESTS, HD), f32),
        pltpu.VMEM((hit_count, REQUESTS, TOK, HEADS, HD), bf16),
        pltpu.VMEM((hit_count, REQUESTS, HD), f32),
    ] + [dma((n,))] * 6 + [dma((int(math.log2(n)),))] * 2 + [dma((5,))]


def solution(mesh):
    n = mesh.shape["cache"]

    def body(prefix_len, hits, span_block, queries, fresh_keys, fresh_values, cache_keys, cache_values):
        hit_count = hits.shape[1]
        vmem = pl.BlockSpec(memory_space=pltpu.VMEM)
        smem = pl.BlockSpec(memory_space=pltpu.SMEM)
        hbm = pl.BlockSpec(memory_space=pltpu.HBM)
        if hit_count == 1 and n // 2 == CAP * PLANE:
            program, scratch, shape = functools.partial(relay_kernel, n), relay_scratch(n), (PER_DEV, HEADS * HD)
        else:
            program, scratch = functools.partial(kernel, n, hit_count), direct_scratch(n, hit_count)
            shape = (PER_DEV, HEADS, HD)
        result = pl.pallas_call(
            program,
            out_shape=pltpu.VMEM(shape, jnp.bfloat16),
            in_specs=[smem, smem, vmem, hbm, hbm, hbm, hbm, hbm],
            out_specs=vmem,
            scratch_shapes=scratch,
            compiler_params=pltpu.CompilerParams(
                collective_id=0, has_side_effects=True, vmem_limit_bytes=60 << 20),
        )(prefix_len, hits.reshape(-1), span_block, queries, fresh_keys, fresh_values, cache_keys, cache_values)
        return result.reshape(PER_DEV, HEADS * HD)

    in_specs = (
        P("groups"), P("groups", None), P("groups", None),
        P(("groups", "cache"), None), P(("groups", "cache"), None), P(("groups", "cache"), None),
        P(("groups", "cache"), None), P(("groups", "cache"), None),
    )
    return jax.shard_map(body, mesh=mesh, in_specs=in_specs,
                         out_specs=P(("groups", "cache"), None), check_vma=False)
```
